256 devices in a mesh: head: 8 (over z), outer: 2 (over core), inner: 16 (over y, x).
Axes of the slice: x: 4, y: 4, z: 8, core: 2. Of those that a mesh axis runs over, the one named last changes fastest.
Arguments:
- query: bfloat16 [8192, 64, 128], P(('outer', 'inner'), 'head'), may hold values from -24 to 24
- keys: bfloat16 [8192, 8, 128], P(('outer', 'inner'), 'head'), may hold values from -8 to 8
- values: bfloat16 [8192, 8, 128], P(('outer', 'inner'), 'head'), may hold values from -6 to 6
- forward_output: bfloat16 [8192, 64, 128], P(('outer', 'inner'), 'head'), may hold values from -2.390625 to 2.390625
- d_out: bfloat16 [8192, 64, 128], P(('outer', 'inner'), 'head'), may hold values from -2.390625 to 2.390625
- span_order: int32 [1, 32], replicated, may hold values from 0 to 31, each once within a row
Outputs:
- d_query: bfloat16 [32, 256, 64, 128], P(('outer', 'inner'), 'head')
- key_gradient: bfloat16 [32, 256, 8, 128], P(('outer', 'inner'), 'head')
- value_gradient: bfloat16 [32, 256, 8, 128], P(('outer', 'inner'), 'head')
The draws below stay inside these ranges and needn't reach their ends.
Inputs may be any that keep to these rules, and one draw needn't show every extreme that they name: `span_order`: each row holds every number once.
All inputs are finite; a program needn't handle non-finite values.
Results may differ from the reference program's by a relative error of at most 0.0051.
Values may be sent and summed in bfloat16 or wider, within the bound.
A program may use at most 64 MiB of HBM per device.

```python
import jax
import jax.numpy as jnp
from jax import lax

QUERY_HEADS = 64
KEY_VALUE_HEADS = 8
HEAD_SIZE = 128
BLOCK_ROWS = 256
SEQUENCE_BLOCKS = 32
SEQUENCE_COUNT = 1
SEQUENCE_TOKENS = 8192


def draw_keys(key, part):
    row_total = SEQUENCE_COUNT * SEQUENCE_TOKENS
    sampled_rows = jnp.clip(jax.random.normal(jax.random.fold_in(key, 19), (row_total, KEY_VALUE_HEADS, HEAD_SIZE), jnp.float32), -8.0, 8.0)
    return sampled_rows.astype(jnp.bfloat16)


def draw_query(key, part):
    row_total = SEQUENCE_COUNT * SEQUENCE_TOKENS
    sampled_rows = jnp.clip(jax.random.normal(jax.random.fold_in(key, 29), (row_total, QUERY_HEADS, HEAD_SIZE), jnp.float32), -8.0, 8.0)
    return sampled_rows.astype(jnp.bfloat16)


def block_levels(stream_key, extent, cuts, smallest, largest):
    level, own = 1.0, jax.random.fold_in(stream_key, 6)
    for dim, parts in cuts:
        draws = jnp.exp(jax.random.uniform(jax.random.fold_in(own, dim), (parts,), jnp.float32, smallest / len(cuts), largest / len(cuts)))
        level = level * jnp.repeat(draws, extent[dim] // parts).reshape([-1 if axis == dim else 1 for axis in range(len(extent))])
    return level


def normal_values(rng, shape, deviation, limit, pieces=(), kind=jnp.bfloat16):
    result = jax.random.normal(rng, shape, jnp.float32) * deviation
    if len(pieces) > 0:
        result = block_levels(rng, shape, pieces, -0.22, 0.18) * result
    return jnp.clip(result, min=-limit, max=limit).astype(kind)


def setup_inputs(seed: int = 0) -> dict:
    streams_of = jax.random.split(jax.random.key(seed), 7)
    return {
        "query": draw_query(jax.random.fold_in(streams_of[6], 71), 0),
        "keys": draw_keys(jax.random.fold_in(streams_of[6], 71), 0),
        "values": normal_values(streams_of[2], (SEQUENCE_COUNT * SEQUENCE_TOKENS, KEY_VALUE_HEADS, HEAD_SIZE), 1.0, 6.0, ((0, 32), (1, 8))),
        "forward_output": normal_values(streams_of[3], (SEQUENCE_COUNT * SEQUENCE_TOKENS, QUERY_HEADS, HEAD_SIZE), 0.3, 2.390625, ((0, 32), (1, 8))),
        "d_out": normal_values(streams_of[4], (SEQUENCE_COUNT * SEQUENCE_TOKENS, QUERY_HEADS, HEAD_SIZE), 0.3, 2.390625, ((0, 32), (1, 8))),
        "span_order": jax.vmap(lambda own: jax.random.permutation(own, SEQUENCE_BLOCKS))(jax.random.split(streams_of[5], SEQUENCE_COUNT)).reshape((SEQUENCE_COUNT, SEQUENCE_BLOCKS)).astype(jnp.int32),
    }


def one_sequence(block_pieces):
    query, keys, values, forward_output, d_out, order_row = block_pieces
    score_scale = HEAD_SIZE ** -0.5
    group_members = QUERY_HEADS // KEY_VALUE_HEADS
    offsets = jnp.arange(BLOCK_ROWS, dtype=jnp.int32)
    position = (order_row[:, None] * BLOCK_ROWS + offsets[None, :]).reshape(SEQUENCE_TOKENS)
    visible = position[None, :] <= position[:, None]
    delta_all = jnp.sum(d_out.astype(jnp.float32) * forward_output.astype(jnp.float32), axis=-1)

    def one_head(head_id):
        group_id = head_id // group_members
        query_head = lax.dynamic_index_in_dim(query, head_id, 1, keepdims=False)
        key_head = lax.dynamic_index_in_dim(keys, group_id, 1, keepdims=False)
        value_head = lax.dynamic_index_in_dim(values, group_id, 1, keepdims=False)
        grad_head = lax.dynamic_index_in_dim(d_out, head_id, 1, keepdims=False)
        delta_head = lax.dynamic_index_in_dim(delta_all, head_id, 1, keepdims=False)
        scores = jnp.dot(query_head, key_head.T, preferred_element_type=jnp.float32) * score_scale
        scores = jnp.where(visible, scores, -jnp.inf)
        highest = jnp.max(scores, axis=1, keepdims=True)
        log_total = highest + jnp.log(jnp.sum(jnp.exp(scores - highest), axis=1, keepdims=True))
        weights = jnp.exp(scores - log_total)
        weights_low = weights.astype(jnp.bfloat16)
        d_weights = jnp.dot(grad_head, value_head.T, preferred_element_type=jnp.float32)
        d_scores = (weights * (d_weights - delta_head[:, None])).astype(jnp.bfloat16)
        grad_query = jnp.dot(d_scores, key_head, preferred_element_type=jnp.float32) * score_scale
        key_gradient_fn = jnp.dot(d_scores.T, query_head, preferred_element_type=jnp.float32) * score_scale
        value_gradient_fn = jnp.dot(weights_low.T, grad_head, preferred_element_type=jnp.float32)
        return grad_query, key_gradient_fn, value_gradient_fn

    grad_query, key_gradient_fn, value_gradient_fn = lax.map(one_head, jnp.arange(QUERY_HEADS, dtype=jnp.int32))
    grad_query = jnp.transpose(grad_query, (1, 0, 2))
    key_gradient_fn = jnp.transpose(jnp.sum(key_gradient_fn.reshape(KEY_VALUE_HEADS, group_members, SEQUENCE_TOKENS, HEAD_SIZE), axis=1), (1, 0, 2))
    value_gradient_fn = jnp.transpose(jnp.sum(value_gradient_fn.reshape(KEY_VALUE_HEADS, group_members, SEQUENCE_TOKENS, HEAD_SIZE), axis=1), (1, 0, 2))
    return (grad_query.astype(jnp.bfloat16), key_gradient_fn.astype(jnp.bfloat16), value_gradient_fn.astype(jnp.bfloat16))


def reference(query, keys, values, forward_output, d_out, span_order):
    block_pieces = (query.reshape(SEQUENCE_COUNT, SEQUENCE_TOKENS, QUERY_HEADS, HEAD_SIZE), keys.reshape(SEQUENCE_COUNT, SEQUENCE_TOKENS, KEY_VALUE_HEADS, HEAD_SIZE),
              values.reshape(SEQUENCE_COUNT, SEQUENCE_TOKENS, KEY_VALUE_HEADS, HEAD_SIZE), forward_output.reshape(SEQUENCE_COUNT, SEQUENCE_TOKENS, QUERY_HEADS, HEAD_SIZE),
              d_out.reshape(SEQUENCE_COUNT, SEQUENCE_TOKENS, QUERY_HEADS, HEAD_SIZE), span_order)
    grad_query, key_gradient_fn, value_gradient_fn = lax.map(one_sequence, block_pieces)
    d_query = grad_query.reshape(SEQUENCE_COUNT * SEQUENCE_BLOCKS, BLOCK_ROWS, QUERY_HEADS, HEAD_SIZE)
    key_gradient = key_gradient_fn.reshape(SEQUENCE_COUNT * SEQUENCE_BLOCKS, BLOCK_ROWS, KEY_VALUE_HEADS, HEAD_SIZE)
    value_gradient = value_gradient_fn.reshape(SEQUENCE_COUNT * SEQUENCE_BLOCKS, BLOCK_ROWS, KEY_VALUE_HEADS, HEAD_SIZE)
    return (d_query, key_gradient, value_gradient)
```

```python
import functools

import jax
import jax.numpy as jnp
from jax import lax
from jax.experimental import pallas as pl
from jax.experimental.pallas import tpu as pltpu
from jax.sharding import PartitionSpec as P

NB, RB, HD, PIECE, QC = 32, 256, 128, 64, 256
NG = NB * PIECE // QC
PER = QC // PIECE
NT = (((1,), (1,)), ((), ()))
TN = (((0,), (0,)), ((), ()))
NN = (((1,), (0,)), ((), ()))
F32, BF16 = jnp.float32, jnp.bfloat16
NEG = -1e30
SCALE = HD ** -0.5
SCALE2 = SCALE * 1.4426950408889634


def dot(a, b, dims):
    return lax.dot_general(a, b, dims, preferred_element_type=F32)


def fill_positions(inv, q_ref, do_ref, dl_ref, qpos, dopos, dlpos):
    for p in range(NB):
        c = inv[p]
        qpos[p * PIECE:(p + 1) * PIECE, :] = q_ref[c].reshape(PIECE, HD)
        dopos[p * PIECE:(p + 1) * PIECE, :] = do_ref[c].reshape(PIECE, HD)
    for p in range(0, NB, 2):
        both = jnp.concatenate([dl_ref[inv[p]][:, :PIECE], dl_ref[inv[p + 1]][:, :PIECE]], axis=1)
        g, off = divmod(p * PIECE, QC)
        dlpos[g, :, off:off + 128] = both


def make_visible(me, shape, shift):
    j = lax.broadcasted_iota(jnp.int32, shape, 1)
    u = lax.broadcasted_iota(jnp.int32, shape, 0)
    row = (j // PIECE) * RB + ((j % PIECE) // 8) * NB + me
    return u + shift <= row


def grads_kernel(variant, inv, me_ref, q_ref, do_ref, dl_ref, kv_ref, dq_ref, dkv_ref,
                 qpos, dopos, dlpos, lse, dqacc, dkacc, dvacc):
    me = me_ref[0]
    fill_positions(inv, q_ref, do_ref, dl_ref, qpos, dopos, dlpos)

    def fold(state, s):
        m, l = state
        s3 = s.reshape(s.shape[0] // 8, 8, QC)
        mn = jnp.maximum(m, jnp.max(s3, axis=0))
        l = l * jnp.exp2(m - mn) + jnp.sum(jnp.exp2(s3 - mn[None]), axis=0)
        return mn, l

    def chunk_total(g, _):
        qg = qpos[pl.ds(pl.multiple_of(g * QC, QC), QC), :]
        state = (jnp.full((8, QC), NEG, F32), jnp.zeros((8, QC), F32))

        def four(t, state):
            for e in range(PER):
                state = fold(state, dot(kv_ref[slot_of(inv[t * PER + e]), 0], qg, NT) * SCALE2)
            return state
        state = lax.fori_loop(0, g, four, state)
        for e in range(PER):
            s = dot(kv_ref[slot_of(inv[g * PER + e]), 0], qg, NT) * SCALE2
            state = fold(state, jnp.where(make_visible(me, s.shape, e * RB), s, NEG))
        m, l = state
        top = jnp.max(m, axis=0, keepdims=True)
        lse[g] = top + jnp.log2(jnp.sum(l * jnp.exp2(m - top), axis=0, keepdims=True))
        return 0
    lax.fori_loop(0, NG, chunk_total, 0)

    dqacc[...] = jnp.zeros_like(dqacc)

    def key_block(p, _):
        c = slot_of(inv[p])
        kb, vb = kv_ref[c, 0], kv_ref[c, 1]
        first = p // PER
        if variant == "T":
            kt = kb.T

        def visit(g, masked):
            rows = pl.ds(pl.multiple_of(g * QC, QC), QC)
            qg, dog = qpos[rows, :], dopos[rows, :]
            s = dot(kb, qg, NT) * SCALE2 - lse[g]
            w = jnp.exp2(s)
            if masked:
                w = jnp.where(make_visible(me, s.shape, (p - g * PER) * RB), w, 0.0)
            dv = dot(w.astype(BF16), dog, NN)
            ds = (w * (dot(vb, dog, NT) - dlpos[g])).astype(BF16)
            dk = dot(ds, qg, NN)
            if variant == "T":
                dqacc[g] += dot(kt, ds, NN)
            else:
                dqacc[g] += dot(ds, kb, TN)
            return dk, dv
        dk, dv = visit(first, True)
        dkacc[...] = dk
        dvacc[...] = dv

        def rest(g, _):
            dk, dv = visit(g, False)
            dkacc[...] += dk
            dvacc[...] += dv
            return 0
        lax.fori_loop(first + 1, NG, rest, 0)
        dkv_ref[c, 0] = (dkacc[...] * SCALE).astype(BF16)
        dkv_ref[c, 1] = dvacc[...].astype(BF16)
        return 0
    lax.fori_loop(0, NB, key_block, 0)

    for p in range(NB):
        g, e = divmod(p, PER)
        if variant == "T":
            if e == 0:
                whole = dqacc[g].T
            part = whole[e * PIECE:(e + 1) * PIECE, :]
        else:
            part = dqacc[g, e * PIECE:(e + 1) * PIECE, :]
        dq_ref[inv[p]] = (part * SCALE).astype(BF16)


def grads(variant, inv, me, q, do, dl, kv):
    acc = (NG, HD, QC) if variant == "T" else (NG, QC, HD)
    vm = pl.BlockSpec(memory_space=pltpu.VMEM)
    sm = pl.BlockSpec(memory_space=pltpu.SMEM)
    return pl.pallas_call(
        functools.partial(grads_kernel, variant),
        out_shape=(jax.ShapeDtypeStruct((NB, PIECE, HD), BF16),
                   jax.ShapeDtypeStruct((NB, 2, RB, HD), BF16)),
        in_specs=[sm, sm, vm, vm, vm, vm],
        out_specs=(vm, vm),
        scratch_shapes=[
            pltpu.VMEM((NB * PIECE, HD), BF16), pltpu.VMEM((NB * PIECE, HD), BF16), pltpu.VMEM((NG, 1, QC), F32),
            pltpu.VMEM((NG, 1, QC), F32), pltpu.VMEM(acc, F32),
            pltpu.VMEM((RB, HD), F32), pltpu.VMEM((RB, HD), F32)],
        compiler_params=pltpu.CompilerParams(vmem_limit_bytes=60 << 20),
        name="grads_" + variant,
    )(inv, me, q, do, dl, kv)


MESH = pl.DeviceIdType.MESH


def place():
    core = lax.axis_index("outer")
    inner = lax.axis_index("inner")
    y, x = inner // 4, lax.rem(inner, 4)
    return core, x + core * (y - x), y + core * (x - y)


def chip_at(core, a, b):
    return a + core * (4 * a + b - a) + (1 - core) * 4 * b


def slot_of(c):
    core, inner = c // 16, c % 16
    y, x = inner // 4, inner % 4
    return core * 16 + 4 * (x + core * (y - x)) + y + core * (x - y)


def turn(v, step):
    return lax.rem(v + step + 4, 4)


def greet(with_heads):
    me = lax.axis_index("outer") * 16 + lax.axis_index("inner")
    barrier = pltpu.get_barrier_semaphore()

    def one(n, _):
        to = lax.rem(me + n, NB)
        pl.semaphore_signal(barrier, inc=1, device_id={"outer": to // 16, "inner": lax.rem(to, 16)}, device_id_type=MESH)
        return 0
    lax.fori_loop(1, NB, one, 0)
    count = NB - 1
    if with_heads:
        z = lax.axis_index("head")

        def head(n, _):
            pl.semaphore_signal(barrier, inc=1, device_id={"head": lax.rem(z + n, 8)}, device_id_type=MESH)
            return 0
        lax.fori_loop(1, 8, head, 0)
        count += 7
    pl.semaphore_wait(barrier, count)
    return me


def wait_bytes(ref, sem):
    pltpu.make_async_copy(ref, ref, sem).wait()


def spread_kernel(k_ref, v_ref, q_ref, do_ref, dl_ref, kv_ref, qo_ref, doo_ref, dlo_ref,
                  kv_send, kv_recv, sib_send, sib_recv, row_send, row_recv, own_sem):
    core, al, be = place()
    me = greet(False)

    def slot(a, b):
        return core * 16 + turn(al, a) * 4 + turn(be, b)

    def to(a, b):
        return {"inner": chip_at(core, turn(al, a), turn(be, b))}
    mine = slot(0, 0)
    own = [pltpu.make_async_copy(k_ref, kv_ref.at[mine, 0], own_sem.at[0]),
           pltpu.make_async_copy(v_ref, kv_ref.at[mine, 1], own_sem.at[1]),
           pltpu.make_async_copy(q_ref.at[:, me], qo_ref.at[me], own_sem.at[2]),
           pltpu.make_async_copy(do_ref.at[:, me], doo_ref.at[me], own_sem.at[3]),
           pltpu.make_async_copy(dl_ref.at[me], dlo_ref.at[me], own_sem.at[4])]
    for c in own:
        c.start()
    own[0].wait()
    own[1].wait()
    started = []

    def send(ref, n, dev):
        c = pltpu.make_async_remote_copy(src_ref=ref, dst_ref=ref, send_sem=kv_send.at[n], recv_sem=kv_recv.at[n],
                                         device_id=dev, device_id_type=MESH)
        c.start()
        started.append(c)

    def arrived(ref, n):
        wait_bytes(ref, kv_recv.at[n])

    def to_sibling(a, b):
        n = turn(al, a) * 4 + turn(be, b)
        c = pltpu.make_async_remote_copy(
            src_ref=kv_ref.at[slot(a, b)], dst_ref=kv_ref.at[slot(a, b)], send_sem=sib_send.at[n], recv_sem=sib_recv.at[n],
            device_id={"outer": 1 - core}, device_id_type=MESH)
        c.start()
        started.append(c)

    def whole(a, b):
        return kv_ref.at[slot(a, b)]

    def half(a, b, h):
        return kv_ref.at[slot(a, b), h]
    send(whole(0, 0), 0, to(1, 0))
    send(whole(0, 0), 1, to(-1, 0))
    send(whole(0, 0), 4, to(0, 1))
    send(whole(0, 0), 5, to(0, -1))
    to_sibling(0, 0)

    def rows(n, _):
        other = lax.rem(me + n, NB)
        dev = {"outer": other // 16, "inner": lax.rem(other, 16)}
        for j, (src, dst) in enumerate(((q_ref.at[:, other], qo_ref), (do_ref.at[:, other], doo_ref), (dl_ref.at[other], dlo_ref))):
            pltpu.make_async_remote_copy(src_ref=src, dst_ref=dst.at[me], send_sem=row_send.at[j], recv_sem=row_recv.at[j],
                                         device_id=dev, device_id_type=MESH).start()
        return 0

    arrived(whole(-1, 0), 0)
    send(half(-1, 0, 0), 2, to(1, 0))
    send(whole(-1, 0), 8, to(0, 1))
    send(whole(-1, 0), 9, to(0, -1))
    to_sibling(-1, 0)
    arrived(whole(1, 0), 1)
    send(half(1, 0, 1), 3, to(-1, 0))
    send(whole(1, 0), 12, to(0, 1))
    send(whole(1, 0), 13, to(0, -1))
    to_sibling(1, 0)
    lax.fori_loop(1, NB, rows, 0)
    base = {0: 4, -1: 8, 1: 12, 2: 16}
    for a in (0, -1, 1, 2):
        n = base[a]
        if a == 2:
            arrived(half(2, 0, 0), 2)
            arrived(half(2, 0, 1), 3)
            send(whole(2, 0), 16, to(0, 1))
            send(whole(2, 0), 17, to(0, -1))
            to_sibling(2, 0)
        arrived(whole(a, -1), n)
        send(half(a, -1, 0), n + 2, to(0, 1))
        to_sibling(a, -1)
        arrived(whole(a, 1), n + 1)
        send(half(a, 1, 1), n + 3, to(0, -1))
        to_sibling(a, 1)
    for a in (0, -1, 1, 2):
        arrived(half(a, 2, 0), base[a] + 2)
        arrived(half(a, 2, 1), base[a] + 3)
        to_sibling(a, 2)
    for n in range(16):
        wait_bytes(kv_ref.at[(1 - core) * 16 + n], sib_recv.at[n])
    for c in started:
        c.wait_send()
    for j, ref in enumerate((qo_ref, doo_ref, dlo_ref)):
        wait_bytes(ref.at[pl.ds(0, NB - 1)], row_recv.at[j])
        wait_bytes(ref.at[pl.ds(0, NB - 1)], row_send.at[j])
    for c in own[2:]:
        c.wait()


def spread(k, v, q, do, dl):
    vm = pl.BlockSpec(memory_space=pltpu.VMEM)
    dma = pltpu.SemaphoreType.DMA
    return pl.pallas_call(
        spread_kernel,
        out_shape=(jax.ShapeDtypeStruct((NB, 2, RB, HD), BF16), jax.ShapeDtypeStruct((NB, 8, 8, HD), BF16),
                   jax.ShapeDtypeStruct((NB, 8, 8, HD), BF16), jax.ShapeDtypeStruct((NB, 1, HD), F32)),
        in_specs=[vm] * 5, out_specs=(vm,) * 4,
        scratch_shapes=[dma((20,)), dma((20,)), dma((16,)), dma((16,)), dma((3,)), dma((3,)), dma((5,))],
        compiler_params=pltpu.CompilerParams(collective_id=0, has_side_effects=True, vmem_limit_bytes=40 << 20),
        name="spread",
    )(k, v, q, do, dl)


def total(*parts):
    out = parts[0].astype(F32)
    for p in parts[1:]:
        out = out + p.astype(F32)
    return out


def collect_kernel(dq_ref, dkv_ref, oq_ref, okv_ref, sib, sums, from_a, opp_a, line, from_b, opp_b, mid, fin, dz,
                   sib_send, sib_recv, a_send, a_recv, b_send, b_recv, z_send, z_recv, x_send, x_recv, own_sem):
    core, al, be = place()
    z = lax.axis_index("head")
    me = greet(True)
    started = []

    def remote(src, dst, ssem, rsem, dev):
        c = pltpu.make_async_remote_copy(src_ref=src, dst_ref=dst, send_sem=ssem, recv_sem=rsem,
                                         device_id=dev, device_id_type=MESH)
        c.start()
        started.append(c)

    def to(a, b):
        return {"inner": chip_at(core, turn(al, a), turn(be, b))}
    order = (2, 1, -1, 0)
    s_al = be
    for n, a in enumerate(order):
        unit = turn(s_al, a)
        remote(dkv_ref.at[pl.ds((1 - core) * 16 + unit * 4, 4)], sib.at[n], sib_send.at[n], sib_recv.at[n], {"outer": 1 - core})

    def heads(n, _):
        other = lax.rem(z + n, 8)
        pltpu.make_async_remote_copy(src_ref=dq_ref.at[:, other], dst_ref=dz.at[:, z], send_sem=z_send.at[0],
                                     recv_sem=z_recv.at[0], device_id={"head": other}, device_id_type=MESH).start()
        return 0
    lax.fori_loop(1, 8, heads, 0)
    own_q = pltpu.make_async_copy(dq_ref.at[:, z], dz.at[:, z], own_sem.at[0])
    own_q.start()

    def mine(a):
        return dkv_ref[pl.ds(core * 16 + turn(al, a) * 4, 4)]
    wait_bytes(sib.at[0], sib_recv.at[0])
    sums[0] = total(mine(2), sib[0]).astype(BF16)
    remote(sums.at[0, :, 0], opp_a.at[0], a_send.at[0], a_recv.at[0], to(1, 0))
    remote(sums.at[0, :, 1], opp_a.at[1], a_send.at[1], a_recv.at[1], to(-1, 0))
    wait_bytes(sib.at[1], sib_recv.at[1])
    wait_bytes(sib.at[2], sib_recv.at[2])
    first, second = mine(1), mine(-1)
    sums[1, :, 1] = total(first[:, 1], sib[1, :, 1]).astype(BF16)
    sums[2, :, 0] = total(second[:, 0], sib[2, :, 0]).astype(BF16)
    wait_bytes(opp_a.at[0], a_recv.at[0])
    sums[1, :, 0] = total(first[:, 0], sib[1, :, 0], opp_a[0]).astype(BF16)
    remote(sums.at[1], from_a.at[0], a_send.at[2], a_recv.at[2], to(1, 0))
    wait_bytes(opp_a.at[1], a_recv.at[1])
    sums[2, :, 1] = total(second[:, 1], sib[2, :, 1], opp_a[1]).astype(BF16)
    remote(sums.at[2], from_a.at[1], a_send.at[3], a_recv.at[3], to(-1, 0))
    wait_bytes(sib.at[3], sib_recv.at[3])
    line[...] = total(mine(0), sib[3])
    wait_bytes(dz.at[:, pl.ds(0, 7)], z_recv.at[0])
    own_q.wait()

    def rows(n, _):
        other = lax.rem(me + n, NB)
        pltpu.make_async_remote_copy(src_ref=dz.at[other], dst_ref=oq_ref.at[me], send_sem=x_send.at[0],
                                     recv_sem=x_recv.at[0], device_id={"outer": other // 16, "inner": lax.rem(other, 16)},
                                     device_id_type=MESH).start()
        return 0
    lax.fori_loop(1, NB, rows, 0)
    own_r = pltpu.make_async_copy(dz.at[me], oq_ref.at[me], own_sem.at[1])
    own_r.start()
    wait_bytes(from_a.at[0], a_recv.at[2])
    wait_bytes(from_a.at[1], a_recv.at[3])

    def strip(b):
        n = turn(be, b)
        return line[n] + from_a[0, n].astype(F32) + from_a[1, n].astype(F32)
    mid[0] = strip(2).astype(BF16)
    remote(mid.at[0, 0], opp_b.at[0], b_send.at[0], b_recv.at[0], to(0, 1))
    remote(mid.at[0, 1], opp_b.at[1], b_send.at[1], b_recv.at[1], to(0, -1))
    up, down, here = strip(1), strip(-1), strip(0)
    wait_bytes(opp_b.at[0], b_recv.at[0])
    mid[1, 0] = (up[0] + opp_b[0].astype(F32)).astype(BF16)
    mid[1, 1] = up[1].astype(BF16)
    remote(mid.at[1], from_b.at[0], b_send.at[2], b_recv.at[2], to(0, 1))
    wait_bytes(opp_b.at[1], b_recv.at[1])
    mid[2, 0] = down[0].astype(BF16)
    mid[2, 1] = (down[1] + opp_b[1].astype(F32)).astype(BF16)
    remote(mid.at[2], from_b.at[1], b_send.at[3], b_recv.at[3], to(0, -1))
    wait_bytes(from_b.at[0], b_recv.at[2])
    wait_bytes(from_b.at[1], b_recv.at[3])
    fin[...] = total(here, from_b[0], from_b[1]).astype(BF16)

    def strips(n, _):
        other = lax.rem(z + n, 8)
        pltpu.make_async_remote_copy(src_ref=fin.at[:, pl.ds(pl.multiple_of(other * 32, 32), 32)], dst_ref=okv_ref.at[z],
                                     send_sem=z_send.at[1], recv_sem=z_recv.at[1], device_id={"head": other},
                                     device_id_type=MESH).start()
        return 0
    lax.fori_loop(1, 8, strips, 0)
    own_k = pltpu.make_async_copy(fin.at[:, pl.ds(pl.multiple_of(z * 32, 32), 32)], okv_ref.at[z], own_sem.at[2])
    own_k.start()
    for c in started:
        c.wait_send()
    wait_bytes(dz.at[:, pl.ds(0, 7)], z_send.at[0])
    wait_bytes(oq_ref.at[pl.ds(0, NB - 1)], x_send.at[0])
    wait_bytes(oq_ref.at[pl.ds(0, NB - 1)], x_recv.at[0])
    wait_bytes(okv_ref.at[pl.ds(0, 7)], z_send.at[1])
    wait_bytes(okv_ref.at[pl.ds(0, 7)], z_recv.at[1])
    own_r.wait()
    own_k.wait()


def collect(dq, dkv):
    vm = pl.BlockSpec(memory_space=pltpu.VMEM)
    dma = pltpu.SemaphoreType.DMA
    block = (2, RB, HD)
    return pl.pallas_call(
        collect_kernel,
        out_shape=(jax.ShapeDtypeStruct((NB, 8, 8, HD), BF16), jax.ShapeDtypeStruct((8, 2, 32, HD), BF16)),
        in_specs=[vm] * 2, out_specs=(vm,) * 2,
        scratch_shapes=[
            pltpu.VMEM((4, 4) + block, BF16), pltpu.VMEM((3, 4) + block, BF16), pltpu.VMEM((2, 4) + block, BF16),
            pltpu.VMEM((2, 4, RB, HD), BF16), pltpu.VMEM((4,) + block, F32), pltpu.VMEM((2,) + block, BF16),
            pltpu.VMEM((2, RB, HD), BF16), pltpu.VMEM((3,) + block, BF16), pltpu.VMEM(block, BF16),
            pltpu.VMEM((NB, 8, 8, HD), BF16),
            dma((4,)), dma((4,)), dma((4,)), dma((4,)), dma((4,)), dma((4,)), dma((2,)), dma((2,)), dma((1,)), dma((1,)),
            dma((3,))],
        compiler_params=pltpu.CompilerParams(collective_id=1, has_side_effects=True, vmem_limit_bytes=48 << 20),
        name="collect",
    )(dq, dkv)


OI = ("outer", "inner")


def body(query, keys, values, forward_output, d_out, span_order):
    inv = jnp.zeros((NB,), jnp.int32).at[span_order[0]].set(jnp.arange(NB, dtype=jnp.int32))
    me = (lax.axis_index("outer") * 16 + lax.axis_index("inner")).astype(jnp.int32).reshape(1)
    delta = jnp.sum(d_out.astype(F32) * forward_output.astype(F32), axis=-1)
    delta = jnp.transpose(delta.reshape(8, NB, 8), (1, 0, 2)).reshape(NB, 1, PIECE)
    delta = jnp.pad(delta, ((0, 0), (0, 0), (0, 128 - PIECE)))
    kv, q, do, dl = spread(keys.reshape(RB, HD), values.reshape(RB, HD), query.reshape(8, NB, 8, HD),
                           d_out.reshape(8, NB, 8, HD), delta)
    dq, dkv = grads("T", inv, me, q, do, dl, kv)
    oq, okv = collect(dq.reshape(NB, 8, 8, HD), dkv)
    okv = jnp.transpose(okv, (1, 2, 0, 3))
    return oq.reshape(1, 32, 64, HD), okv[0][None], okv[1][None]


def solution(mesh):
    rows = P(OI, "head", None)
    out = P(OI, "head", None, None)
    return jax.shard_map(body, mesh=mesh, in_specs=(rows,) * 5 + (P(),), out_specs=(out,) * 3, check_vma=False)
```

```python
import jax
import jax.numpy as jnp
from jax import lax
from jax.experimental import pallas as pl
from jax.experimental.pallas import tpu as pltpu
from jax.sharding import PartitionSpec as P

NB, RB, HD, PIECE, QC, KEYS = 32, 256, 128, 64, 512, 4
NG = NB * PIECE // QC
PER = QC // PIECE
NT = (((1,), (1,)), ((), ()))
TN = (((0,), (0,)), ((), ()))
NN = (((1,), (0,)), ((), ()))
F32, BF16 = jnp.float32, jnp.bfloat16
NEG = -1e30
SCALE = HD ** -0.5
SCALE2 = SCALE * 1.4426950408889634


def dot(a, b, dims):
    return lax.dot_general(a, b, dims, preferred_element_type=F32)


def fill_positions(inv, q_ref, do_ref, dl_ref, qpos, dopos, dlpos):
    for p in range(NB):
        c = inv[p]
        qpos[p * PIECE:(p + 1) * PIECE, :] = q_ref[c].reshape(PIECE, HD)
        dopos[p * PIECE:(p + 1) * PIECE, :] = do_ref[c].reshape(PIECE, HD)
    for p in range(0, NB, 2):
        both = jnp.concatenate([dl_ref[inv[p]][:, :PIECE], dl_ref[inv[p + 1]][:, :PIECE]], axis=1)
        g, off = divmod(p * PIECE, QC)
        dlpos[g, :, off:off + 128] = both


def make_visible(me, shape, shift):
    j = lax.broadcasted_iota(jnp.int32, shape, 1)
    u = lax.broadcasted_iota(jnp.int32, shape, 0)
    row = (j // PIECE) * RB + ((j % PIECE) // 8) * NB + me
    return u + shift <= row


def grads_kernel(order, q_ref, do_ref, dl_ref, kv_ref, dq_ref, dkv_ref,
                 qpos, dopos, dlpos, lse, dqacc, kpos, vpos, dkacc, dvacc, inv):
    me = lax.axis_index("outer") * 16 + lax.axis_index("inner")
    for c in range(NB):
        inv[order[c]] = c
    fill_positions(inv, q_ref, do_ref, dl_ref, qpos, dopos, dlpos)
    for p in range(NB):
        c = slot_of(inv[p])
        kpos[p * RB:(p + 1) * RB, :] = kv_ref[c, 0]
        vpos[p * RB:(p + 1) * RB, :] = kv_ref[c, 1]

    def keys_at(ref, p, count):
        return ref[pl.ds(pl.multiple_of(p * RB, RB), count * RB), :]

    def fold(state, s):
        m, l = state
        s3 = s.reshape(s.shape[0] // 8, 8, s.shape[1])
        mn = jnp.maximum(m, jnp.max(s3, axis=0))
        low = mn * SCALE2
        l = l * jnp.exp2(m * SCALE2 - low) + jnp.sum(jnp.exp2(s3 * SCALE2 - low[None]), axis=0)
        return mn, l

    def chunk_total(g, _):
        qg = qpos[pl.ds(pl.multiple_of(g * QC, QC), QC), :]
        state = (jnp.full((8, QC), NEG, F32), jnp.zeros((8, QC), F32))

        def some(t, state):
            return fold(state, dot(keys_at(kpos, t * KEYS, KEYS), qg, NT))
        state = lax.fori_loop(0, g * PER // KEYS, some, state)
        half = PER // 2
        for e in range(0, half, KEYS):
            s = dot(keys_at(kpos, g * PER + e, KEYS), qg, NT)
            state = fold(state, jnp.where(make_visible(me, s.shape, e * RB), s, NEG))

        def settle(m, l):
            top = jnp.max(m, axis=0, keepdims=True)
            return top * SCALE2 + jnp.log2(jnp.sum(l * jnp.exp2((m - top) * SCALE2), axis=0, keepdims=True))
        m, l = state
        lse[g, :, :QC // 2] = settle(m[:, :QC // 2], l[:, :QC // 2])
        state = (m[:, QC // 2:], l[:, QC // 2:])
        for e in range(0, half, KEYS):
            s = dot(keys_at(kpos, g * PER + half + e, KEYS), qg[QC // 2:], NT)
            state = fold(state, jnp.where(make_visible(me, s.shape, e * RB), s, NEG))
        lse[g, :, QC // 2:] = settle(*state)
        return 0
    lax.fori_loop(0, NG, chunk_total, 0)

    dqacc[...] = jnp.zeros_like(dqacc)

    def key_block(t, _):
        p = t * KEYS
        kb, vb = keys_at(kpos, p, KEYS), keys_at(vpos, p, KEYS)
        first = p // PER
        kt = kb.T

        def visit(g, lo, masked):
            rows = pl.ds(pl.multiple_of(g * QC + lo, QC // 2), QC - lo)
            qg, dog = qpos[rows, :], dopos[rows, :]
            s = dot(kb, qg, NT) * SCALE2 - lse[g, :, lo:]
            w = jnp.exp2(s)
            if masked:
                w = jnp.where(make_visible(me, s.shape, 0), w, 0.0)
            dv = dot(w.astype(BF16), dog, NN)
            ds = (w * (dot(vb, dog, NT) - dlpos[g, :, lo:])).astype(BF16)
            dk = dot(ds, qg, NN)
            dqacc[g, :, lo:] += dot(kt, ds, NN)
            return dk, dv

        @pl.when(t % 2 == 0)
        def _():
            dkacc[...], dvacc[...] = visit(first, 0, True)

        @pl.when(t % 2 == 1)
        def _():
            dkacc[...], dvacc[...] = visit(first, QC // 2, True)

        def rest(g, _):
            dk, dv = visit(g, 0, False)
            dkacc[...] += dk
            dvacc[...] += dv
            return 0
        lax.fori_loop(first + 1, NG, rest, 0)
        for e in range(KEYS):
            c = slot_of(inv[p + e])
            dkv_ref[c, 0] = (dkacc[e * RB:(e + 1) * RB, :] * SCALE).astype(BF16)
            dkv_ref[c, 1] = dvacc[e * RB:(e + 1) * RB, :].astype(BF16)
        return 0
    lax.fori_loop(0, NB // KEYS, key_block, 0)

    for p in range(NB):
        g, e = divmod(p, PER)
        if e == 0:
            whole = dqacc[g].T
        dq_ref[inv[p]] = (whole[e * PIECE:(e + 1) * PIECE, :] * SCALE).astype(BF16)


def grads(order, q, do, dl, kv):
    vm = pl.BlockSpec(memory_space=pltpu.VMEM)
    sm = pl.BlockSpec(memory_space=pltpu.SMEM)
    return pl.pallas_call(
        grads_kernel,
        out_shape=(jax.ShapeDtypeStruct((NB, PIECE, HD), BF16), jax.ShapeDtypeStruct((NB, 2, RB, HD), BF16)),
        in_specs=[sm, vm, vm, vm, vm],
        out_specs=(vm, vm),
        scratch_shapes=[
            pltpu.VMEM((NB * PIECE, HD), BF16), pltpu.VMEM((NB * PIECE, HD), BF16), pltpu.VMEM((NG, 1, QC), F32),
            pltpu.VMEM((NG, 1, QC), F32), pltpu.VMEM((NG, HD, QC), F32),
            pltpu.VMEM((NB * RB, HD), BF16), pltpu.VMEM((NB * RB, HD), BF16),
            pltpu.VMEM((KEYS * RB, HD), F32), pltpu.VMEM((KEYS * RB, HD), F32), pltpu.SMEM((NB,), jnp.int32)],
        compiler_params=pltpu.CompilerParams(vmem_limit_bytes=40 << 20),
        name="grads",
    )(order, q, do, dl, kv)


MESH = pl.DeviceIdType.MESH


def place():
    core = lax.axis_index("outer")
    inner = lax.axis_index("inner")
    y, x = inner // 4, lax.rem(inner, 4)
    return core, x + core * (y - x), y + core * (x - y)


def chip_at(core, a, b):
    return a + core * (4 * a + b - a) + (1 - core) * 4 * b


def slot_of(c):
    core, inner = c // 16, c % 16
    y, x = inner // 4, inner % 4
    return core * 16 + 4 * (x + core * (y - x)) + y + core * (x - y)


def turn(v, step):
    return lax.rem(v + step + 4, 4)


def greet(with_heads):
    me = lax.axis_index("outer") * 16 + lax.axis_index("inner")
    barrier = pltpu.get_barrier_semaphore()

    def one(n, _):
        to = lax.rem(me + n, NB)
        pl.semaphore_signal(barrier, inc=1, device_id={"outer": to // 16, "inner": lax.rem(to, 16)}, device_id_type=MESH)
        return 0
    lax.fori_loop(1, NB, one, 0)
    count = NB - 1
    if with_heads:
        z = lax.axis_index("head")

        def head(n, _):
            pl.semaphore_signal(barrier, inc=1, device_id={"head": lax.rem(z + n, 8)}, device_id_type=MESH)
            return 0
        lax.fori_loop(1, 8, head, 0)
        count += 7
    pl.semaphore_wait(barrier, count)
    return me


def wait_bytes(ref, sem):
    pltpu.make_async_copy(ref, ref, sem).wait()


def spread_kernel(k_ref, v_ref, q_ref, do_ref, dl_ref, kv_ref, qo_ref, doo_ref, dlo_ref,
                  kv_send, kv_recv, sib_send, sib_recv, row_send, row_recv, own_sem):
    core, al, be = place()
    me = greet(False)

    def slot(a, b):
        return core * 16 + turn(al, a) * 4 + turn(be, b)

    def to(a, b):
        return {"inner": chip_at(core, turn(al, a), turn(be, b))}
    mine = slot(0, 0)
    own = [pltpu.make_async_copy(k_ref, kv_ref.at[mine, 0], own_sem.at[0]),
           pltpu.make_async_copy(v_ref, kv_ref.at[mine, 1], own_sem.at[1]),
           pltpu.make_async_copy(q_ref.at[:, me], qo_ref.at[me], own_sem.at[2]),
           pltpu.make_async_copy(do_ref.at[:, me], doo_ref.at[me], own_sem.at[3]),
           pltpu.make_async_copy(dl_ref.at[me], dlo_ref.at[me], own_sem.at[4])]
    for c in own:
        c.start()
    own[0].wait()
    own[1].wait()
    started = []

    def send(ref, n, dev):
        c = pltpu.make_async_remote_copy(src_ref=ref, dst_ref=ref, send_sem=kv_send.at[n], recv_sem=kv_recv.at[n],
                                         device_id=dev, device_id_type=MESH)
        c.start()
        started.append(c)

    def arrived(ref, n):
        wait_bytes(ref, kv_recv.at[n])

    def to_sibling(a, b):
        n = turn(al, a) * 4 + turn(be, b)
        c = pltpu.make_async_remote_copy(
            src_ref=kv_ref.at[slot(a, b)], dst_ref=kv_ref.at[slot(a, b)], send_sem=sib_send.at[n], recv_sem=sib_recv.at[n],
            device_id={"outer": 1 - core}, device_id_type=MESH)
        c.start()
        started.append(c)

    def whole(a, b):
        return kv_ref.at[slot(a, b)]

    def half(a, b, h):
        return kv_ref.at[slot(a, b), h]
    send(whole(0, 0), 0, to(1, 0))
    send(whole(0, 0), 1, to(-1, 0))
    send(whole(0, 0), 4, to(0, 1))
    send(whole(0, 0), 5, to(0, -1))
    to_sibling(0, 0)

    def rows(n, _):
        other = lax.rem(me + n, NB)
        dev = {"outer": other // 16, "inner": lax.rem(other, 16)}
        for j, (src, dst) in enumerate(((q_ref.at[:, other], qo_ref), (do_ref.at[:, other], doo_ref), (dl_ref.at[other], dlo_ref))):
            pltpu.make_async_remote_copy(src_ref=src, dst_ref=dst.at[me], send_sem=row_send.at[j], recv_sem=row_recv.at[j],
                                         device_id=dev, device_id_type=MESH).start()
        return 0

    arrived(whole(-1, 0), 0)
    send(half(-1, 0, 0), 2, to(1, 0))
    send(whole(-1, 0), 8, to(0, 1))
    send(whole(-1, 0), 9, to(0, -1))
    to_sibling(-1, 0)
    arrived(whole(1, 0), 1)
    send(half(1, 0, 1), 3, to(-1, 0))
    send(whole(1, 0), 12, to(0, 1))
    send(whole(1, 0), 13, to(0, -1))
    to_sibling(1, 0)
    lax.fori_loop(1, NB, rows, 0)
    base = {0: 4, -1: 8, 1: 12, 2: 16}
    for a in (0, -1, 1, 2):
        n = base[a]
        if a == 2:
            arrived(half(2, 0, 0), 2)
            arrived(half(2, 0, 1), 3)
            send(whole(2, 0), 16, to(0, 1))
            send(whole(2, 0), 17, to(0, -1))
            to_sibling(2, 0)
        arrived(whole(a, -1), n)
        send(half(a, -1, 0), n + 2, to(0, 1))
        to_sibling(a, -1)
        arrived(whole(a, 1), n + 1)
        send(half(a, 1, 1), n + 3, to(0, -1))
        to_sibling(a, 1)
    for a in (0, -1, 1, 2):
        arrived(half(a, 2, 0), base[a] + 2)
        arrived(half(a, 2, 1), base[a] + 3)
        to_sibling(a, 2)
    for n in range(16):
        wait_bytes(kv_ref.at[(1 - core) * 16 + n], sib_recv.at[n])
    for c in started:
        c.wait_send()
    for j, ref in enumerate((qo_ref, doo_ref, dlo_ref)):
        wait_bytes(ref.at[pl.ds(0, NB - 1)], row_recv.at[j])
        wait_bytes(ref.at[pl.ds(0, NB - 1)], row_send.at[j])
    for c in own[2:]:
        c.wait()


def spread(k, v, q, do, dl):
    vm = pl.BlockSpec(memory_space=pltpu.VMEM)
    dma = pltpu.SemaphoreType.DMA
    return pl.pallas_call(
        spread_kernel,
        out_shape=(jax.ShapeDtypeStruct((NB, 2, RB, HD), BF16), jax.ShapeDtypeStruct((NB, 8, 8, HD), BF16),
                   jax.ShapeDtypeStruct((NB, 8, 8, HD), BF16), jax.ShapeDtypeStruct((NB, 1, HD), F32)),
        in_specs=[pl.BlockSpec(memory_space=pltpu.HBM)] * 4 + [vm], out_specs=(vm,) * 4,
        scratch_shapes=[dma((20,)), dma((20,)), dma((16,)), dma((16,)), dma((3,)), dma((3,)), dma((5,))],
        compiler_params=pltpu.CompilerParams(collective_id=0, has_side_effects=True, vmem_limit_bytes=16 << 20),
        name="spread",
    )(k, v, q, do, dl)


def total(*parts):
    out = parts[0].astype(F32)
    for p in parts[1:]:
        out = out + p.astype(F32)
    return out


def collect_kernel(dq_ref, dkv_ref, oq_ref, okv_ref, sib, sums, from_a, opp_a, line, from_b, opp_b, mid, fin, dz,
                   sib_send, sib_recv, a_send, a_recv, b_send, b_recv, z_send, z_recv, x_send, x_recv, own_sem):
    core, al, be = place()
    z = lax.axis_index("head")
    me = greet(True)
    started = []

    def remote(src, dst, ssem, rsem, dev):
        c = pltpu.make_async_remote_copy(src_ref=src, dst_ref=dst, send_sem=ssem, recv_sem=rsem,
                                         device_id=dev, device_id_type=MESH)
        c.start()
        started.append(c)

    def to(a, b):
        return {"inner": chip_at(core, turn(al, a), turn(be, b))}
    order = (2, 1, -1, 0)
    s_al = be
    for n, a in enumerate(order):
        unit = turn(s_al, a)
        remote(dkv_ref.at[pl.ds((1 - core) * 16 + unit * 4, 4)], sib.at[n], sib_send.at[n], sib_recv.at[n], {"outer": 1 - core})

    def heads(n, _):
        other = lax.rem(z + n, 8)
        pltpu.make_async_remote_copy(src_ref=dq_ref.at[:, other], dst_ref=dz.at[:, z], send_sem=z_send.at[0],
                                     recv_sem=z_recv.at[0], device_id={"head": other}, device_id_type=MESH).start()
        return 0
    lax.fori_loop(1, 8, heads, 0)
    own_q = pltpu.make_async_copy(dq_ref.at[:, z], dz.at[:, z], own_sem.at[0])
    own_q.start()

    def mine(a):
        return dkv_ref[pl.ds(core * 16 + turn(al, a) * 4, 4)]
    wait_bytes(sib.at[0], sib_recv.at[0])
    sums[0] = total(mine(2), sib[0]).astype(BF16)
    remote(sums.at[0, :, 0], opp_a.at[0], a_send.at[0], a_recv.at[0], to(1, 0))
    remote(sums.at[0, :, 1], opp_a.at[1], a_send.at[1], a_recv.at[1], to(-1, 0))
    wait_bytes(sib.at[1], sib_recv.at[1])
    wait_bytes(sib.at[2], sib_recv.at[2])
    first, second = mine(1), mine(-1)
    sums[1, :, 1] = total(first[:, 1], sib[1, :, 1]).astype(BF16)
    sums[2, :, 0] = total(second[:, 0], sib[2, :, 0]).astype(BF16)
    wait_bytes(opp_a.at[0], a_recv.at[0])
    sums[1, :, 0] = total(first[:, 0], sib[1, :, 0], opp_a[0]).astype(BF16)
    remote(sums.at[1], from_a.at[0], a_send.at[2], a_recv.at[2], to(1, 0))
    wait_bytes(opp_a.at[1], a_recv.at[1])
    sums[2, :, 1] = total(second[:, 1], sib[2, :, 1], opp_a[1]).astype(BF16)
    remote(sums.at[2], from_a.at[1], a_send.at[3], a_recv.at[3], to(-1, 0))
    wait_bytes(sib.at[3], sib_recv.at[3])
    line[...] = total(mine(0), sib[3])
    wait_bytes(dz.at[:, pl.ds(0, 7)], z_recv.at[0])
    own_q.wait()

    def rows(n, _):
        other = lax.rem(me + n, NB)
        pltpu.make_async_remote_copy(src_ref=dz.at[other], dst_ref=oq_ref.at[me], send_sem=x_send.at[0],
                                     recv_sem=x_recv.at[0], device_id={"outer": other // 16, "inner": lax.rem(other, 16)},
                                     device_id_type=MESH).start()
        return 0
    lax.fori_loop(1, NB, rows, 0)
    own_r = pltpu.make_async_copy(dz.at[me], oq_ref.at[me], own_sem.at[1])
    own_r.start()
    wait_bytes(from_a.at[0], a_recv.at[2])
    wait_bytes(from_a.at[1], a_recv.at[3])

    def strip(b):
        n = turn(be, b)
        return line[n] + from_a[0, n].astype(F32) + from_a[1, n].astype(F32)
    mid[0] = strip(2).astype(BF16)
    remote(mid.at[0, 0], opp_b.at[0], b_send.at[0], b_recv.at[0], to(0, 1))
    remote(mid.at[0, 1], opp_b.at[1], b_send.at[1], b_recv.at[1], to(0, -1))
    up, down, here = strip(1), strip(-1), strip(0)
    wait_bytes(opp_b.at[0], b_recv.at[0])
    mid[1, 0] = (up[0] + opp_b[0].astype(F32)).astype(BF16)
    mid[1, 1] = up[1].astype(BF16)
    remote(mid.at[1], from_b.at[0], b_send.at[2], b_recv.at[2], to(0, 1))
    wait_bytes(opp_b.at[1], b_recv.at[1])
    mid[2, 0] = down[0].astype(BF16)
    mid[2, 1] = (down[1] + opp_b[1].astype(F32)).astype(BF16)
    remote(mid.at[2], from_b.at[1], b_send.at[3], b_recv.at[3], to(0, -1))
    wait_bytes(from_b.at[0], b_recv.at[2])
    wait_bytes(from_b.at[1], b_recv.at[3])
    fin[...] = total(here, from_b[0], from_b[1]).astype(BF16)

    def strips(n, _):
        other = lax.rem(z + n, 8)
        pltpu.make_async_remote_copy(src_ref=fin.at[:, pl.ds(pl.multiple_of(other * 32, 32), 32)], dst_ref=okv_ref.at[z],
                                     send_sem=z_send.at[1], recv_sem=z_recv.at[1], device_id={"head": other},
                                     device_id_type=MESH).start()
        return 0
    lax.fori_loop(1, 8, strips, 0)
    own_k = pltpu.make_async_copy(fin.at[:, pl.ds(pl.multiple_of(z * 32, 32), 32)], okv_ref.at[z], own_sem.at[2])
    own_k.start()
    for c in started:
        c.wait_send()
    wait_bytes(dz.at[:, pl.ds(0, 7)], z_send.at[0])
    wait_bytes(oq_ref.at[pl.ds(0, NB - 1)], x_send.at[0])
    wait_bytes(oq_ref.at[pl.ds(0, NB - 1)], x_recv.at[0])
    wait_bytes(okv_ref.at[pl.ds(0, 7)], z_send.at[1])
    wait_bytes(okv_ref.at[pl.ds(0, 7)], z_recv.at[1])
    own_r.wait()
    own_k.wait()


def collect(dq, dkv):
    vm = pl.BlockSpec(memory_space=pltpu.VMEM)
    dma = pltpu.SemaphoreType.DMA
    block = (2, RB, HD)
    return pl.pallas_call(
        collect_kernel,
        out_shape=(jax.ShapeDtypeStruct((NB, 8, 8, HD), BF16), jax.ShapeDtypeStruct((8, 2, 32, HD), BF16)),
        in_specs=[vm] * 2, out_specs=(vm,) * 2,
        scratch_shapes=[
            pltpu.VMEM((4, 4) + block, BF16), pltpu.VMEM((3, 4) + block, BF16), pltpu.VMEM((2, 4) + block, BF16),
            pltpu.VMEM((2, 4, RB, HD), BF16), pltpu.VMEM((4,) + block, F32), pltpu.VMEM((2,) + block, BF16),
            pltpu.VMEM((2, RB, HD), BF16), pltpu.VMEM((3,) + block, BF16), pltpu.VMEM(block, BF16),
            pltpu.VMEM((NB, 8, 8, HD), BF16),
            dma((4,)), dma((4,)), dma((4,)), dma((4,)), dma((4,)), dma((4,)), dma((2,)), dma((2,)), dma((1,)), dma((1,)),
            dma((3,))],
        compiler_params=pltpu.CompilerParams(collective_id=1, has_side_effects=True, vmem_limit_bytes=40 << 20),
        name="collect",
    )(dq, dkv)


OI = ("outer", "inner")


def body(query, keys, values, forward_output, d_out, span_order):
    delta = jnp.sum(d_out.astype(F32) * forward_output.astype(F32), axis=-1)
    delta = jnp.transpose(delta.reshape(8, NB, 8), (1, 0, 2)).reshape(NB, 1, PIECE)
    delta = jnp.pad(delta, ((0, 0), (0, 0), (0, 128 - PIECE)))
    kv, q, do, dl = spread(keys.reshape(RB, HD), values.reshape(RB, HD), query.reshape(8, NB, 8, HD),
                           d_out.reshape(8, NB, 8, HD), delta)
    dq, dkv = grads(span_order[0], q, do, dl, kv)
    oq, okv = collect(dq.reshape(NB, 8, 8, HD), dkv)
    okv = jnp.transpose(okv, (1, 2, 0, 3))
    return oq.reshape(1, 32, 64, HD), okv[0][None], okv[1][None]


def solution(mesh):
    rows = P(OI, "head", None)
    out = P(OI, "head", None, None)
    return jax.shard_map(body, mesh=mesh, in_specs=(rows,) * 5 + (P(),), out_specs=(out,) * 3, check_vma=False)
```

```python
import jax
import jax.numpy as jnp
from jax import lax
from jax.experimental import pallas as pl
from jax.experimental.pallas import tpu as pltpu
from jax.sharding import PartitionSpec as P

NB, RB, HD, PIECE, QC, KEYS = 32, 256, 128, 64, 512, 4
NG = NB * PIECE // QC
PER = QC // PIECE
NT = (((1,), (1,)), ((), ()))
TN = (((0,), (0,)), ((), ()))
NN = (((1,), (0,)), ((), ()))
F32, BF16 = jnp.float32, jnp.bfloat16
NEG = -1e30
SCALE = HD ** -0.5
SCALE2 = SCALE * 1.4426950408889634


def dot(a, b, dims):
    return lax.dot_general(a, b, dims, preferred_element_type=F32)


def fill_positions(inv, q_ref, do_ref, dl_ref, qpos, dopos, dlpos):
    for p in range(NB):
        c = inv[p]
        qpos[p * PIECE:(p + 1) * PIECE, :] = q_ref[c].reshape(PIECE, HD)
        dopos[p * PIECE:(p + 1) * PIECE, :] = do_ref[c].reshape(PIECE, HD)
    for p in range(0, NB, 2):
        both = jnp.concatenate([dl_ref[inv[p]][:, :PIECE], dl_ref[inv[p + 1]][:, :PIECE]], axis=1)
        g, off = divmod(p * PIECE, QC)
        dlpos[g, :, off:off + 128] = both


def make_visible(me, shape, shift):
    j = lax.broadcasted_iota(jnp.int32, shape, 1)
    u = lax.broadcasted_iota(jnp.int32, shape, 0)
    row = (j // PIECE) * RB + ((j % PIECE) // 8) * NB + me
    return u + shift <= row


def grads_kernel(order, q_ref, do_ref, dl_ref, kv_ref, dq_ref, dkv_ref,
                 qpos, dopos, dlpos, lse, dqacc, kpos, vpos, dkacc, dvacc, inv):
    me = lax.axis_index("outer") * 16 + lax.axis_index("inner")
    for c in range(NB):
        inv[order[0, c]] = c
    fill_positions(inv, q_ref, do_ref, dl_ref, qpos, dopos, dlpos)
    for p in range(NB):
        c = slot_of(inv[p])
        kpos[p * RB:(p + 1) * RB, :] = kv_ref[c, 0]
        vpos[p * RB:(p + 1) * RB, :] = kv_ref[c, 1]

    def keys_at(ref, p, count):
        return ref[pl.ds(pl.multiple_of(p * RB, RB), count * RB), :]

    def fold(state, s):
        m, l = state
        s3 = s.reshape(s.shape[0] // 8, 8, s.shape[1])
        mn = jnp.maximum(m, jnp.max(s3, axis=0))
        low = mn * SCALE2
        l = l * jnp.exp2(m * SCALE2 - low) + jnp.sum(jnp.exp2(s3 * SCALE2 - low[None]), axis=0)
        return mn, l

    def chunk_total(g, _):
        qg = qpos[pl.ds(pl.multiple_of(g * QC, QC), QC), :]
        state = (jnp.full((8, QC), NEG, F32), jnp.zeros((8, QC), F32))

        def some(t, state):
            return fold(state, dot(keys_at(kpos, t * KEYS, KEYS), qg, NT))
        state = lax.fori_loop(0, g * PER // KEYS, some, state)
        half = PER // 2
        for e in range(0, half, KEYS):
            s = dot(keys_at(kpos, g * PER + e, KEYS), qg, NT)
            state = fold(state, jnp.where(make_visible(me, s.shape, e * RB), s, NEG))

        def settle(m, l):
            top = jnp.max(m, axis=0, keepdims=True)
            return top * SCALE2 + jnp.log2(jnp.sum(l * jnp.exp2((m - top) * SCALE2), axis=0, keepdims=True))
        m, l = state
        lse[g, :, :QC // 2] = settle(m[:, :QC // 2], l[:, :QC // 2])
        state = (m[:, QC // 2:], l[:, QC // 2:])
        for e in range(0, half, KEYS):
            s = dot(keys_at(kpos, g * PER + half + e, KEYS), qg[QC // 2:], NT)
            state = fold(state, jnp.where(make_visible(me, s.shape, e * RB), s, NEG))
        lse[g, :, QC // 2:] = settle(*state)
        return 0
    lax.fori_loop(0, NG, chunk_total, 0)

    dqacc[...] = jnp.zeros_like(dqacc)

    def key_block(t, _):
        p = t * KEYS
        kb, vb = keys_at(kpos, p, KEYS), keys_at(vpos, p, KEYS)
        first = p // PER
        kt = kb.T

        def visit(g, lo, masked):
            rows = pl.ds(pl.multiple_of(g * QC + lo, QC // 2), QC - lo)
            qg, dog = qpos[rows, :], dopos[rows, :]
            s = dot(kb, qg, NT) * SCALE2 - lse[g, :, lo:]
            w = jnp.exp2(s)
            if masked:
                w = jnp.where(make_visible(me, s.shape, 0), w, 0.0)
            dv = dot(w.astype(BF16), dog, NN)
            ds = (w * (dot(vb, dog, NT) - dlpos[g, :, lo:])).astype(BF16)
            dk = dot(ds, qg, NN)
            dqacc[g, :, lo:] += dot(kt, ds, NN)
            return dk, dv

        @pl.when(t % 2 == 0)
        def _():
            dkacc[...], dvacc[...] = visit(first, 0, True)

        @pl.when(t % 2 == 1)
        def _():
            dkacc[...], dvacc[...] = visit(first, QC // 2, True)

        def rest(g, _):
            dk, dv = visit(g, 0, False)
            dkacc[...] += dk
            dvacc[...] += dv
            return 0
        lax.fori_loop(first + 1, NG, rest, 0)
        for e in range(KEYS):
            c = slot_of(inv[p + e])
            dkv_ref[c, 0] = (dkacc[e * RB:(e + 1) * RB, :] * SCALE).astype(BF16)
            dkv_ref[c, 1] = dvacc[e * RB:(e + 1) * RB, :].astype(BF16)
        return 0
    lax.fori_loop(0, NB // KEYS, key_block, 0)

    for p in range(NB):
        g, e = divmod(p, PER)
        if e == 0:
            whole = dqacc[g].T
        dq_ref[inv[p]] = (whole[e * PIECE:(e + 1) * PIECE, :] * SCALE).astype(BF16)


def grads(order, q, do, dl, kv):
    vm = pl.BlockSpec(memory_space=pltpu.VMEM)
    sm = pl.BlockSpec(memory_space=pltpu.SMEM)
    return pl.pallas_call(
        grads_kernel,
        out_shape=(jax.ShapeDtypeStruct((NB, PIECE, HD), BF16), jax.ShapeDtypeStruct((NB, 2, RB, HD), BF16)),
        in_specs=[sm, vm, vm, vm, vm],
        out_specs=(vm, vm),
        scratch_shapes=[
            pltpu.VMEM((NB * PIECE, HD), BF16), pltpu.VMEM((NB * PIECE, HD), BF16), pltpu.VMEM((NG, 1, QC), F32),
            pltpu.VMEM((NG, 1, QC), F32), pltpu.VMEM((NG, HD, QC), F32),
            pltpu.VMEM((NB * RB, HD), BF16), pltpu.VMEM((NB * RB, HD), BF16),
            pltpu.VMEM((KEYS * RB, HD), F32), pltpu.VMEM((KEYS * RB, HD), F32), pltpu.SMEM((NB,), jnp.int32)],
        compiler_params=pltpu.CompilerParams(vmem_limit_bytes=40 << 20),
        name="grads",
    )(order, q, do, dl, kv)


MESH = pl.DeviceIdType.MESH


def place():
    core = lax.axis_index("outer")
    inner = lax.axis_index("inner")
    y, x = inner // 4, lax.rem(inner, 4)
    return core, x + core * (y - x), y + core * (x - y)


def chip_at(core, a, b):
    return a + core * (4 * a + b - a) + (1 - core) * 4 * b


def slot_of(c):
    core, inner = c // 16, c % 16
    y, x = inner // 4, inner % 4
    return core * 16 + 4 * (x + core * (y - x)) + y + core * (x - y)


def turn(v, step):
    return lax.rem(v + step + 4, 4)


def greet(with_heads):
    me = lax.axis_index("outer") * 16 + lax.axis_index("inner")
    barrier = pltpu.get_barrier_semaphore()

    def one(n, _):
        to = lax.rem(me + n, NB)
        pl.semaphore_signal(barrier, inc=1, device_id={"outer": to // 16, "inner": lax.rem(to, 16)}, device_id_type=MESH)
        return 0
    lax.fori_loop(1, NB, one, 0)
    count = NB - 1
    if with_heads:
        z = lax.axis_index("head")

        def head(n, _):
            pl.semaphore_signal(barrier, inc=1, device_id={"head": lax.rem(z + n, 8)}, device_id_type=MESH)
            return 0
        lax.fori_loop(1, 8, head, 0)
        count += 7
    pl.semaphore_wait(barrier, count)
    return me


def wait_bytes(ref, sem):
    pltpu.make_async_copy(ref, ref, sem).wait()


def spread_kernel(own_kv_ref, own_rows_ref, dl_ref, kv_ref, qo_ref, doo_ref, dlo_ref,
                  kv_send, kv_recv, sib_send, sib_recv, row_send, row_recv, own_sem):
    core, al, be = place()
    me = greet(False)
    k_ref, v_ref, q_ref, do_ref = own_kv_ref.at[0], own_kv_ref.at[1], own_rows_ref.at[0], own_rows_ref.at[1]

    def slot(a, b):
        return core * 16 + turn(al, a) * 4 + turn(be, b)

    def to(a, b):
        return {"inner": chip_at(core, turn(al, a), turn(be, b))}
    mine = slot(0, 0)
    own = [pltpu.make_async_copy(k_ref, kv_ref.at[mine, 0], own_sem.at[0]),
           pltpu.make_async_copy(v_ref, kv_ref.at[mine, 1], own_sem.at[1]),
           pltpu.make_async_copy(q_ref.at[:, me], qo_ref.at[me], own_sem.at[2]),
           pltpu.make_async_copy(do_ref.at[:, me], doo_ref.at[me], own_sem.at[3]),
           pltpu.make_async_copy(dl_ref.at[me], dlo_ref.at[me], own_sem.at[4])]
    for c in own:
        c.start()
    own[0].wait()
    own[1].wait()
    started = []

    def send(ref, n, dev):
        c = pltpu.make_async_remote_copy(src_ref=ref, dst_ref=ref, send_sem=kv_send.at[n], recv_sem=kv_recv.at[n],
                                         device_id=dev, device_id_type=MESH)
        c.start()
        started.append(c)

    def arrived(ref, n):
        wait_bytes(ref, kv_recv.at[n])

    def to_sibling(a, b):
        n = turn(al, a) * 4 + turn(be, b)
        c = pltpu.make_async_remote_copy(
            src_ref=kv_ref.at[slot(a, b)], dst_ref=kv_ref.at[slot(a, b)], send_sem=sib_send.at[n], recv_sem=sib_recv.at[n],
            device_id={"outer": 1 - core}, device_id_type=MESH)
        c.start()
        started.append(c)

    def whole(a, b):
        return kv_ref.at[slot(a, b)]

    def half(a, b, h):
        return kv_ref.at[slot(a, b), h]
    send(whole(0, 0), 0, to(1, 0))
    send(whole(0, 0), 1, to(-1, 0))
    send(whole(0, 0), 4, to(0, 1))
    send(whole(0, 0), 5, to(0, -1))
    to_sibling(0, 0)

    def rows(n, _):
        other = lax.rem(me + n, NB)
        dev = {"outer": other // 16, "inner": lax.rem(other, 16)}
        for j, (src, dst) in enumerate(((q_ref.at[:, other], qo_ref), (do_ref.at[:, other], doo_ref), (dl_ref.at[other], dlo_ref))):
            pltpu.make_async_remote_copy(src_ref=src, dst_ref=dst.at[me], send_sem=row_send.at[j], recv_sem=row_recv.at[j],
                                         device_id=dev, device_id_type=MESH).start()
        return 0

    lax.fori_loop(1, 9, rows, 0)
    arrived(whole(-1, 0), 0)
    send(half(-1, 0, 0), 2, to(1, 0))
    send(whole(-1, 0), 8, to(0, 1))
    send(whole(-1, 0), 9, to(0, -1))
    to_sibling(-1, 0)
    arrived(whole(1, 0), 1)
    send(half(1, 0, 1), 3, to(-1, 0))
    send(whole(1, 0), 12, to(0, 1))
    send(whole(1, 0), 13, to(0, -1))
    to_sibling(1, 0)
    lax.fori_loop(9, 17, rows, 0)
    base = {0: 4, -1: 8, 1: 12, 2: 16}
    for a in (0, -1, 1, 2):
        n = base[a]
        if a == 2:
            arrived(half(2, 0, 0), 2)
            arrived(half(2, 0, 1), 3)
            send(whole(2, 0), 16, to(0, 1))
            send(whole(2, 0), 17, to(0, -1))
            to_sibling(2, 0)
        if a in (-1, 1):
            lax.fori_loop(17 if a < 0 else 25, 25 if a < 0 else NB, rows, 0)
        arrived(whole(a, -1), n)
        send(half(a, -1, 0), n + 2, to(0, 1))
        to_sibling(a, -1)
        arrived(whole(a, 1), n + 1)
        send(half(a, 1, 1), n + 3, to(0, -1))
        to_sibling(a, 1)
    for a in (0, -1, 1, 2):
        arrived(half(a, 2, 0), base[a] + 2)
        arrived(half(a, 2, 1), base[a] + 3)
        to_sibling(a, 2)
    for n in range(16):
        wait_bytes(kv_ref.at[(1 - core) * 16 + n], sib_recv.at[n])
    for c in started:
        c.wait_send()
    for j, ref in enumerate((qo_ref, doo_ref, dlo_ref)):
        wait_bytes(ref.at[pl.ds(0, NB - 1)], row_recv.at[j])
        wait_bytes(ref.at[pl.ds(0, NB - 1)], row_send.at[j])
    for c in own[2:]:
        c.wait()


def spread(own_kv, own_rows, dl):
    vm = pl.BlockSpec(memory_space=pltpu.VMEM)
    dma = pltpu.SemaphoreType.DMA
    return pl.pallas_call(
        spread_kernel,
        out_shape=(jax.ShapeDtypeStruct((NB, 2, RB, HD), BF16), jax.ShapeDtypeStruct((NB, 8, 8, HD), BF16),
                   jax.ShapeDtypeStruct((NB, 8, 8, HD), BF16), jax.ShapeDtypeStruct((NB, 1, HD), F32)),
        in_specs=[vm] * 3, out_specs=(vm,) * 4,
        scratch_shapes=[dma((20,)), dma((20,)), dma((16,)), dma((16,)), dma((3,)), dma((3,)), dma((5,))],
        compiler_params=pltpu.CompilerParams(collective_id=0, has_side_effects=True, vmem_limit_bytes=16 << 20),
        name="spread",
    )(own_kv, own_rows, dl)


def total(*parts):
    out = parts[0].astype(F32)
    for p in parts[1:]:
        out = out + p.astype(F32)
    return out


def collect_kernel(dq_ref, dkv_ref, oq_ref, okv_ref, sib, sums, from_a, opp_a, line, from_b, opp_b, mid, fin, dz,
                   sib_send, sib_recv, a_send, a_recv, b_send, b_recv, z_send, z_recv, x_send, x_recv, own_sem):
    core, al, be = place()
    z = lax.axis_index("head")
    me = greet(True)
    inner = lax.rem(me, 16)
    started = []

    def remote(src, dst, ssem, rsem, dev):
        c = pltpu.make_async_remote_copy(src_ref=src, dst_ref=dst, send_sem=ssem, recv_sem=rsem,
                                         device_id=dev, device_id_type=MESH)
        c.start()
        started.append(c)

    def to(a, b):
        return {"inner": chip_at(core, turn(al, a), turn(be, b))}
    order = (2, 1, -1, 0)

    def to_sibling(i, j):
        slot = (1 - core) * 16 + turn(be, order[i]) * 4 + turn(al, order[j])
        n = i * 4 + j
        remote(dkv_ref.at[slot], sib.at[n], sib_send.at[n], sib_recv.at[n], {"outer": 1 - core})
    for j in range(4):
        to_sibling(0, j)

    def heads(h):
        def one(n, _):
            other = lax.rem(z + n, 8)
            part = pl.ds(h * 16, 16)
            pltpu.make_async_remote_copy(src_ref=dq_ref.at[part, other], dst_ref=dz.at[part, z], send_sem=z_send.at[h],
                                         recv_sem=z_recv.at[h], device_id={"head": other}, device_id_type=MESH).start()
            return 0
        lax.fori_loop(1, 8, one, 0)
    heads(0)
    for j in range(4):
        to_sibling(1, j)
        to_sibling(2, j)
    heads(1)
    for j in range(4):
        to_sibling(3, j)
    own_q = pltpu.make_async_copy(dq_ref.at[:, z], dz.at[:, z], own_sem.at[0])
    own_q.start()

    def mine(i, j):
        return dkv_ref[core * 16 + turn(al, order[i]) * 4 + turn(be, order[j])]

    def rows(h):
        wait_bytes(dz.at[pl.ds(0, 16), pl.ds(0, 7)], z_recv.at[h])

        def one(n, _):
            other = lax.rem(inner + n, 16)
            pltpu.make_async_remote_copy(src_ref=dz.at[h * 16 + other], dst_ref=oq_ref.at[me], send_sem=x_send.at[0],
                                         recv_sem=x_recv.at[0], device_id={"outer": h, "inner": other},
                                         device_id_type=MESH).start()
            return 0
        lax.fori_loop(core if h else 1 - core, 16, one, 0)

    def sibling_in(i, j):
        wait_bytes(sib.at[i * 4 + j], sib_recv.at[i * 4 + j])
    for j in range(4):
        sibling_in(0, j)
        sums[0, j] = total(mine(0, j), sib[j]).astype(BF16)
        remote(sums.at[0, j, 0], opp_a.at[0, j], a_send.at[j], a_recv.at[j], to(1, 0))
        remote(sums.at[0, j, 1], opp_a.at[1, j], a_send.at[4 + j], a_recv.at[4 + j], to(-1, 0))
    for j in range(4):
        for i in (1, 2):
            sibling_in(i, j)
            h = i - 1
            own = mine(i, j)
            sums[i, j, 1 - h] = total(own[1 - h], sib[i * 4 + j, 1 - h]).astype(BF16)
            wait_bytes(opp_a.at[h, j], a_recv.at[4 * h + j])
            sums[i, j, h] = total(own[h], sib[i * 4 + j, h], opp_a[h, j]).astype(BF16)
            n = 8 + 4 * h + j
            remote(sums.at[i, j], from_a.at[h, j], a_send.at[n], a_recv.at[n], to(1 - 2 * h, 0))
    for j in range(4):
        sibling_in(3, j)
        line[j] = total(mine(3, j), sib[12 + j])
    own_q.wait()
    rows(0)

    def strip(j):
        wait_bytes(from_a.at[0, j], a_recv.at[8 + j])
        wait_bytes(from_a.at[1, j], a_recv.at[12 + j])
        return total(line[j], from_a[0, j], from_a[1, j])
    mid[0] = strip(0).astype(BF16)
    remote(mid.at[0, 0], opp_b.at[0], b_send.at[0], b_recv.at[0], to(0, 1))
    remote(mid.at[0, 1], opp_b.at[1], b_send.at[1], b_recv.at[1], to(0, -1))
    for i in (1, 2):
        h = i - 1
        whole = strip(i)
        mid[i, 1 - h] = whole[1 - h].astype(BF16)
        wait_bytes(opp_b.at[h], b_recv.at[h])
        mid[i, h] = total(whole[h], opp_b[h]).astype(BF16)
        remote(mid.at[i], from_b.at[h], b_send.at[2 + h], b_recv.at[2 + h], to(0, 1 - 2 * h))
    line[3] = strip(3)
    wait_bytes(from_b.at[0], b_recv.at[2])
    wait_bytes(from_b.at[1], b_recv.at[3])
    fin[...] = total(line[3], from_b[0], from_b[1]).astype(BF16)

    def strips(n, _):
        other = lax.rem(z + n, 8)
        pltpu.make_async_remote_copy(src_ref=fin.at[:, pl.ds(pl.multiple_of(other * 32, 32), 32)], dst_ref=okv_ref.at[z],
                                     send_sem=z_send.at[2], recv_sem=z_recv.at[2], device_id={"head": other},
                                     device_id_type=MESH).start()
        return 0
    lax.fori_loop(1, 8, strips, 0)
    own_k = pltpu.make_async_copy(fin.at[:, pl.ds(pl.multiple_of(z * 32, 32), 32)], okv_ref.at[z], own_sem.at[2])
    own_k.start()
    rows(1)
    own_r = pltpu.make_async_copy(dz.at[me], oq_ref.at[me], own_sem.at[1])
    own_r.start()
    for c in started:
        c.wait_send()
    for h in range(2):
        wait_bytes(dz.at[pl.ds(0, 16), pl.ds(0, 7)], z_send.at[h])
    wait_bytes(oq_ref.at[pl.ds(0, NB - 1)], x_send.at[0])
    wait_bytes(oq_ref.at[pl.ds(0, NB - 1)], x_recv.at[0])
    wait_bytes(okv_ref.at[pl.ds(0, 7)], z_send.at[2])
    wait_bytes(okv_ref.at[pl.ds(0, 7)], z_recv.at[2])
    own_r.wait()
    own_k.wait()


def collect(dq, dkv):
    vm = pl.BlockSpec(memory_space=pltpu.VMEM)
    dma = pltpu.SemaphoreType.DMA
    block = (2, RB, HD)
    return pl.pallas_call(
        collect_kernel,
        out_shape=(jax.ShapeDtypeStruct((NB, 8, 8, HD), BF16), jax.ShapeDtypeStruct((8, 2, 32, HD), BF16)),
        in_specs=[vm] * 2, out_specs=(vm,) * 2,
        scratch_shapes=[
            pltpu.VMEM((16,) + block, BF16), pltpu.VMEM((3, 4) + block, BF16), pltpu.VMEM((2, 4) + block, BF16),
            pltpu.VMEM((2, 4, RB, HD), BF16), pltpu.VMEM((4,) + block, F32), pltpu.VMEM((2,) + block, BF16),
            pltpu.VMEM((2, RB, HD), BF16), pltpu.VMEM((3,) + block, BF16), pltpu.VMEM(block, BF16),
            pltpu.VMEM((NB, 8, 8, HD), BF16),
            dma((16,)), dma((16,)), dma((16,)), dma((16,)), dma((4,)), dma((4,)), dma((3,)), dma((3,)), dma((1,)), dma((1,)),
            dma((3,))],
        compiler_params=pltpu.CompilerParams(collective_id=1, has_side_effects=True, vmem_limit_bytes=40 << 20),
        name="collect",
    )(dq, dkv)


OI = ("outer", "inner")


def body(query, keys, values, forward_output, d_out, span_order):
    delta = jnp.sum(d_out.astype(F32) * forward_output.astype(F32), axis=-1)
    delta = jnp.transpose(delta.reshape(8, NB, 8), (1, 0, 2)).reshape(NB, 1, PIECE)
    delta = jnp.pad(delta, ((0, 0), (0, 0), (0, 128 - PIECE)))
    own_kv = jnp.stack([keys.reshape(RB, HD), values.reshape(RB, HD)])
    own_rows = jnp.stack([query, d_out]).reshape(2, 8, NB, 8, HD)
    kv, q, do, dl = spread(own_kv, own_rows, delta)
    dq, dkv = grads(span_order, q, do, dl, kv)
    oq, okv = collect(dq.reshape(NB, 8, 8, HD), dkv)
    okv = jnp.transpose(okv, (1, 2, 0, 3))
    return oq.reshape(1, 32, 64, HD), okv[0][None], okv[1][None]


def solution(mesh):
    rows = P(OI, "head", None)
    out = P(OI, "head", None, None)
    return jax.shard_map(body, mesh=mesh, in_specs=(rows,) * 5 + (P(),), out_specs=(out,) * 3, check_vma=False)
```

```python
import jax
import jax.numpy as jnp
from jax import lax
from jax.experimental import pallas as pl
from jax.experimental.pallas import tpu as pltpu
from jax.sharding import PartitionSpec as P

NB, RB, HD, PIECE, QC, KEYS = 32, 256, 128, 64, 512, 4
NG = NB * PIECE // QC
PER = QC // PIECE
NT = (((1,), (1,)), ((), ()))
TN = (((0,), (0,)), ((), ()))
NN = (((1,), (0,)), ((), ()))
F32, BF16 = jnp.float32, jnp.bfloat16
NEG = -1e30
SCALE = HD ** -0.5
SCALE2 = SCALE * 1.4426950408889634


def dot(a, b, dims):
    return lax.dot_general(a, b, dims, preferred_element_type=F32)


def fill_positions(inv, q_ref, do_ref, dl_ref, qpos, dopos, dlpos):
    for p in range(NB):
        c = inv[p]
        qpos[p * PIECE:(p + 1) * PIECE, :] = q_ref[c].reshape(PIECE, HD)
        dopos[p * PIECE:(p + 1) * PIECE, :] = do_ref[c].reshape(PIECE, HD)
    for p in range(0, NB, 2):
        both = jnp.concatenate([dl_ref[inv[p]][:, :PIECE], dl_ref[inv[p + 1]][:, :PIECE]], axis=1)
        g, off = divmod(p * PIECE, QC)
        dlpos[g, :, off:off + 128] = both


def make_visible(me, shape, shift):
    j = lax.broadcasted_iota(jnp.int32, shape, 1)
    u = lax.broadcasted_iota(jnp.int32, shape, 0)
    row = (j // PIECE) * RB + ((j % PIECE) // 8) * NB + me
    return u + shift <= row


def grads_kernel(order, q_ref, do_ref, dl_ref, kv_ref, dq_ref, dkv_ref,
                 qpos, dopos, dlpos, lse, dqacc, kpos, vpos, dkacc, dvacc, inv):
    me = lax.axis_index("outer") * 16 + lax.axis_index("inner")
    for c in range(NB):
        inv[order[0, c]] = c
    fill_positions(inv, q_ref, do_ref, dl_ref, qpos, dopos, dlpos)
    for p in range(NB):
        c = slot_of(inv[p])
        kpos[p * RB:(p + 1) * RB, :] = kv_ref[c, 0]
        vpos[p * RB:(p + 1) * RB, :] = kv_ref[c, 1]

    def keys_at(ref, p, count):
        return ref[pl.ds(pl.multiple_of(p * RB, RB), count * RB), :]

    def fold(state, s):
        m, l = state
        s3 = s.reshape(s.shape[0] // 8, 8, s.shape[1])
        mn = jnp.maximum(m, jnp.max(s3, axis=0))
        low = mn * SCALE2
        l = l * jnp.exp2(m * SCALE2 - low) + jnp.sum(jnp.exp2(s3 * SCALE2 - low[None]), axis=0)
        return mn, l

    def chunk_total(g, _):
        qg = qpos[pl.ds(pl.multiple_of(g * QC, QC), QC), :]
        state = (jnp.full((8, QC), NEG, F32), jnp.zeros((8, QC), F32))

        def some(t, state):
            return fold(state, dot(keys_at(kpos, t * KEYS, KEYS), qg, NT))
        state = lax.fori_loop(0, g * PER // KEYS, some, state)
        half = PER // 2
        for e in range(0, half, KEYS):
            s = dot(keys_at(kpos, g * PER + e, KEYS), qg, NT)
            state = fold(state, jnp.where(make_visible(me, s.shape, e * RB), s, NEG))

        def settle(m, l):
            top = jnp.max(m, axis=0, keepdims=True)
            return top * SCALE2 + jnp.log2(jnp.sum(l * jnp.exp2((m - top) * SCALE2), axis=0, keepdims=True))
        m, l = state
        lse[g, :, :QC // 2] = settle(m[:, :QC // 2], l[:, :QC // 2])
        state = (m[:, QC // 2:], l[:, QC // 2:])
        for e in range(0, half, KEYS):
            s = dot(keys_at(kpos, g * PER + half + e, KEYS), qg[QC // 2:], NT)
            state = fold(state, jnp.where(make_visible(me, s.shape, e * RB), s, NEG))
        lse[g, :, QC // 2:] = settle(*state)
        return 0
    lax.fori_loop(0, NG, chunk_total, 0)

    dqacc[...] = jnp.zeros_like(dqacc)

    def key_block(t, _):
        p = t * KEYS
        kb, vb = keys_at(kpos, p, KEYS), keys_at(vpos, p, KEYS)
        first = p // PER
        kt = kb.T

        def visit(g, lo, masked):
            rows = pl.ds(pl.multiple_of(g * QC + lo, QC // 2), QC - lo)
            qg, dog = qpos[rows, :], dopos[rows, :]
            s = dot(kb, qg, NT) * SCALE2 - lse[g, :, lo:]
            w = jnp.exp2(s)
            if masked:
                w = jnp.where(make_visible(me, s.shape, 0), w, 0.0)
            dv = dot(w.astype(BF16), dog, NN)
            ds = (w * (dot(vb, dog, NT) - dlpos[g, :, lo:])).astype(BF16)
            dk = dot(ds, qg, NN)
            dqacc[g, :, lo:] += dot(kt, ds, NN)
            return dk, dv

        @pl.when(t % 2 == 0)
        def _():
            dkacc[...], dvacc[...] = visit(first, 0, True)

        @pl.when(t % 2 == 1)
        def _():
            dkacc[...], dvacc[...] = visit(first, QC // 2, True)

        def rest(g, _):
            dk, dv = visit(g, 0, False)
            dkacc[...] += dk
            dvacc[...] += dv
            return 0
        lax.fori_loop(first + 1, NG, rest, 0)
        for e in range(KEYS):
            c = slot_of(inv[p + e])
            dkv_ref[c, 0] = (dkacc[e * RB:(e + 1) * RB, :] * SCALE).astype(BF16)
            dkv_ref[c, 1] = dvacc[e * RB:(e + 1) * RB, :].astype(BF16)
        return 0
    lax.fori_loop(0, NB // KEYS, key_block, 0)

    for p in range(NB):
        g, e = divmod(p, PER)
        if e == 0:
            whole = dqacc[g].T
        dq_ref[inv[p]] = (whole[e * PIECE:(e + 1) * PIECE, :] * SCALE).astype(BF16)


def grads(order, q, do, dl, kv):
    vm = pl.BlockSpec(memory_space=pltpu.VMEM)
    sm = pl.BlockSpec(memory_space=pltpu.SMEM)
    return pl.pallas_call(
        grads_kernel,
        out_shape=(jax.ShapeDtypeStruct((NB, PIECE, HD), BF16), jax.ShapeDtypeStruct((NB, 2, RB, HD), BF16)),
        in_specs=[sm, vm, vm, vm, vm],
        out_specs=(vm, vm),
        scratch_shapes=[
            pltpu.VMEM((NB * PIECE, HD), BF16), pltpu.VMEM((NB * PIECE, HD), BF16), pltpu.VMEM((NG, 1, QC), F32),
            pltpu.VMEM((NG, 1, QC), F32), pltpu.VMEM((NG, HD, QC), F32),
            pltpu.VMEM((NB * RB, HD), BF16), pltpu.VMEM((NB * RB, HD), BF16),
            pltpu.VMEM((KEYS * RB, HD), F32), pltpu.VMEM((KEYS * RB, HD), F32), pltpu.SMEM((NB,), jnp.int32)],
        compiler_params=pltpu.CompilerParams(vmem_limit_bytes=40 << 20),
        name="grads",
    )(order, q, do, dl, kv)


MESH = pl.DeviceIdType.MESH


def place():
    core = lax.axis_index("outer")
    inner = lax.axis_index("inner")
    y, x = inner // 4, lax.rem(inner, 4)
    return core, x + core * (y - x), y + core * (x - y)


def chip_at(core, a, b):
    return a + core * (4 * a + b - a) + (1 - core) * 4 * b


def slot_of(c):
    core, inner = c // 16, c % 16
    y, x = inner // 4, inner % 4
    return core * 16 + 4 * (x + core * (y - x)) + y + core * (x - y)


def turn(v, step):
    return lax.rem(v + step + 4, 4)


def greet(with_heads):
    me = lax.axis_index("outer") * 16 + lax.axis_index("inner")
    barrier = pltpu.get_barrier_semaphore()

    def one(n, _):
        to = lax.rem(me + n, NB)
        pl.semaphore_signal(barrier, inc=1, device_id={"outer": to // 16, "inner": lax.rem(to, 16)}, device_id_type=MESH)
        return 0
    lax.fori_loop(1, NB, one, 0)
    count = NB - 1
    if with_heads:
        z = lax.axis_index("head")

        def head(n, _):
            pl.semaphore_signal(barrier, inc=1, device_id={"head": lax.rem(z + n, 8)}, device_id_type=MESH)
            return 0
        lax.fori_loop(1, 8, head, 0)
        count += 7
    pl.semaphore_wait(barrier, count)
    return me


def wait_bytes(ref, sem):
    pltpu.make_async_copy(ref, ref, sem).wait()


def spread_kernel(own_kv_ref, own_rows_ref, dl_ref, kv_ref, qo_ref, doo_ref, dlo_ref,
                  kv_send, kv_recv, sib_send, sib_recv, row_send, row_recv, own_sem):
    core, al, be = place()
    me = greet(False)
    k_ref, v_ref, q_ref, do_ref = own_kv_ref.at[0], own_kv_ref.at[1], own_rows_ref.at[0], own_rows_ref.at[1]

    def slot(a, b):
        return core * 16 + turn(al, a) * 4 + turn(be, b)

    def to(a, b):
        return {"inner": chip_at(core, turn(al, a), turn(be, b))}
    mine = slot(0, 0)
    own = [pltpu.make_async_copy(k_ref, kv_ref.at[mine, 0], own_sem.at[0]),
           pltpu.make_async_copy(v_ref, kv_ref.at[mine, 1], own_sem.at[1]),
           pltpu.make_async_copy(q_ref.at[:, me], qo_ref.at[me], own_sem.at[2]),
           pltpu.make_async_copy(do_ref.at[:, me], doo_ref.at[me], own_sem.at[3]),
           pltpu.make_async_copy(dl_ref.at[me], dlo_ref.at[me], own_sem.at[4])]
    for c in own:
        c.start()
    own[0].wait()
    own[1].wait()
    started = []

    def send(ref, n, dev):
        c = pltpu.make_async_remote_copy(src_ref=ref, dst_ref=ref, send_sem=kv_send.at[n], recv_sem=kv_recv.at[n],
                                         device_id=dev, device_id_type=MESH)
        c.start()
        started.append(c)

    def arrived(ref, n):
        wait_bytes(ref, kv_recv.at[n])

    def to_sibling(a, b):
        n = turn(al, a) * 4 + turn(be, b)
        c = pltpu.make_async_remote_copy(
            src_ref=kv_ref.at[slot(a, b)], dst_ref=kv_ref.at[slot(a, b)], send_sem=sib_send.at[n], recv_sem=sib_recv.at[n],
            device_id={"outer": 1 - core}, device_id_type=MESH)
        c.start()
        started.append(c)

    def whole(a, b):
        return kv_ref.at[slot(a, b)]

    def half(a, b, h):
        return kv_ref.at[slot(a, b), h]
    def send_both(a, b, n, dev):
        for h in range(2):
            send(half(a, b, h), 2 * n + h, dev)

    def relay(a, b, n, to_h, to_n, dev, fan=None):
        for h in range(2):
            arrived(half(a, b, h), 2 * n + h)
            if h == to_h:
                send(half(a, b, h), 2 * to_n, dev)
            if fan is not None:
                send(half(a, b, h), 2 * fan + h, to(0, 1))
                send(half(a, b, h), 2 * fan + 2 + h, to(0, -1))
        to_sibling(a, b)
    send_both(0, 0, 0, to(1, 0))
    send_both(0, 0, 1, to(-1, 0))
    send_both(0, 0, 4, to(0, 1))
    send_both(0, 0, 5, to(0, -1))
    to_sibling(0, 0)

    def rows(n, _):
        other = lax.rem(me + n, NB)
        dev = {"outer": other // 16, "inner": lax.rem(other, 16)}
        for j, (src, dst) in enumerate(((q_ref.at[:, other], qo_ref), (do_ref.at[:, other], doo_ref), (dl_ref.at[other], dlo_ref))):
            pltpu.make_async_remote_copy(src_ref=src, dst_ref=dst.at[me], send_sem=row_send.at[j], recv_sem=row_recv.at[j],
                                         device_id=dev, device_id_type=MESH).start()
        return 0

    lax.fori_loop(1, 9, rows, 0)
    relay(-1, 0, 0, 0, 2, to(1, 0), 8)
    relay(1, 0, 1, 1, 3, to(-1, 0), 12)
    lax.fori_loop(9, 17, rows, 0)
    base = {0: 4, -1: 8, 1: 12, 2: 16}
    for a in (0, -1, 1, 2):
        n = base[a]
        if a == 2:
            for h in range(2):
                arrived(half(2, 0, h), 4 + 2 * h)
                send(half(2, 0, h), 32 + h, to(0, 1))
                send(half(2, 0, h), 34 + h, to(0, -1))
            to_sibling(2, 0)
        if a in (-1, 1):
            lax.fori_loop(17 if a < 0 else 25, 25 if a < 0 else NB, rows, 0)
        relay(a, -1, n, 0, n + 2, to(0, 1))
        relay(a, 1, n + 1, 1, n + 3, to(0, -1))
    for a in (0, -1, 1, 2):
        for h in range(2):
            arrived(half(a, 2, h), 2 * (base[a] + 2 + h))
        to_sibling(a, 2)
    for n in range(16):
        wait_bytes(kv_ref.at[(1 - core) * 16 + n], sib_recv.at[n])
    for c in started:
        c.wait_send()
    for j, ref in enumerate((qo_ref, doo_ref, dlo_ref)):
        wait_bytes(ref.at[pl.ds(0, NB - 1)], row_recv.at[j])
        wait_bytes(ref.at[pl.ds(0, NB - 1)], row_send.at[j])
    for c in own[2:]:
        c.wait()


def spread(own_kv, own_rows, dl):
    vm = pl.BlockSpec(memory_space=pltpu.VMEM)
    dma = pltpu.SemaphoreType.DMA
    return pl.pallas_call(
        spread_kernel,
        out_shape=(jax.ShapeDtypeStruct((NB, 2, RB, HD), BF16), jax.ShapeDtypeStruct((NB, 8, 8, HD), BF16),
                   jax.ShapeDtypeStruct((NB, 8, 8, HD), BF16), jax.ShapeDtypeStruct((NB, 1, HD), F32)),
        in_specs=[vm] * 3, out_specs=(vm,) * 4,
        scratch_shapes=[dma((40,)), dma((40,)), dma((16,)), dma((16,)), dma((3,)), dma((3,)), dma((5,))],
        compiler_params=pltpu.CompilerParams(collective_id=0, has_side_effects=True, vmem_limit_bytes=16 << 20),
        name="spread",
    )(own_kv, own_rows, dl)


def total(*parts):
    out = parts[0].astype(F32)
    for p in parts[1:]:
        out = out + p.astype(F32)
    return out


def collect_kernel(dq_ref, dkv_ref, oq_ref, okv_ref, sib, sums, from_a, opp_a, line, from_b, opp_b, mid, fin, dz,
                   sib_send, sib_recv, a_send, a_recv, b_send, b_recv, z_send, z_recv, x_send, x_recv, own_sem):
    core, al, be = place()
    z = lax.axis_index("head")
    me = greet(True)
    inner = lax.rem(me, 16)
    started = []

    def remote(src, dst, ssem, rsem, dev):
        c = pltpu.make_async_remote_copy(src_ref=src, dst_ref=dst, send_sem=ssem, recv_sem=rsem,
                                         device_id=dev, device_id_type=MESH)
        c.start()
        started.append(c)

    def to(a, b):
        return {"inner": chip_at(core, turn(al, a), turn(be, b))}
    order = (2, 1, -1, 0)

    def to_sibling(i, j):
        slot = (1 - core) * 16 + turn(be, order[i]) * 4 + turn(al, order[j])
        n = i * 4 + j
        remote(dkv_ref.at[slot], sib.at[n], sib_send.at[n], sib_recv.at[n], {"outer": 1 - core})
    for j in range(4):
        to_sibling(0, j)

    def heads(h):
        def one(n, _):
            other = lax.rem(z + n, 8)
            part = pl.ds(h * 16, 16)
            pltpu.make_async_remote_copy(src_ref=dq_ref.at[part, other], dst_ref=dz.at[part, z], send_sem=z_send.at[h],
                                         recv_sem=z_recv.at[h], device_id={"head": other}, device_id_type=MESH).start()
            return 0
        lax.fori_loop(1, 8, one, 0)
    heads(0)
    for j in range(4):
        to_sibling(1, j)
        to_sibling(2, j)
    heads(1)
    for j in range(4):
        to_sibling(3, j)
    own_q = pltpu.make_async_copy(dq_ref.at[:, z], dz.at[:, z], own_sem.at[0])
    own_q.start()

    def mine(i, j):
        return dkv_ref[core * 16 + turn(al, order[i]) * 4 + turn(be, order[j])]

    def rows(h):
        wait_bytes(dz.at[pl.ds(0, 16), pl.ds(0, 7)], z_recv.at[h])

        def one(n, _):
            other = lax.rem(inner + n, 16)
            pltpu.make_async_remote_copy(src_ref=dz.at[h * 16 + other], dst_ref=oq_ref.at[me], send_sem=x_send.at[0],
                                         recv_sem=x_recv.at[0], device_id={"outer": h, "inner": other},
                                         device_id_type=MESH).start()
            return 0
        lax.fori_loop(core if h else 1 - core, 16, one, 0)

    def sibling_in(i, j):
        wait_bytes(sib.at[i * 4 + j], sib_recv.at[i * 4 + j])
    for j in range(4):
        sibling_in(0, j)
        sums[0, j] = total(mine(0, j), sib[j]).astype(BF16)
        remote(sums.at[0, j, 0], opp_a.at[0, j], a_send.at[j], a_recv.at[j], to(1, 0))
        remote(sums.at[0, j, 1], opp_a.at[1, j], a_send.at[4 + j], a_recv.at[4 + j], to(-1, 0))
    for j in range(4):
        for i in (1, 2):
            sibling_in(i, j)
            h = i - 1
            own = mine(i, j)
            sums[i, j, 1 - h] = total(own[1 - h], sib[i * 4 + j, 1 - h]).astype(BF16)
            wait_bytes(opp_a.at[h, j], a_recv.at[4 * h + j])
            sums[i, j, h] = total(own[h], sib[i * 4 + j, h], opp_a[h, j]).astype(BF16)
            n = 8 + 4 * h + j
            remote(sums.at[i, j], from_a.at[h, j], a_send.at[n], a_recv.at[n], to(1 - 2 * h, 0))
    for j in range(4):
        sibling_in(3, j)
        line[j] = total(mine(3, j), sib[12 + j])
    own_q.wait()

    def strip(j):
        wait_bytes(from_a.at[0, j], a_recv.at[8 + j])
        wait_bytes(from_a.at[1, j], a_recv.at[12 + j])
        return total(line[j], from_a[0, j], from_a[1, j])
    mid[0] = strip(0).astype(BF16)
    remote(mid.at[0, 0], opp_b.at[0], b_send.at[0], b_recv.at[0], to(0, 1))
    remote(mid.at[0, 1], opp_b.at[1], b_send.at[1], b_recv.at[1], to(0, -1))
    rows(0)
    for i in (1, 2):
        h = i - 1
        whole = strip(i)
        mid[i, 1 - h] = whole[1 - h].astype(BF16)
        wait_bytes(opp_b.at[h], b_recv.at[h])
        mid[i, h] = total(whole[h], opp_b[h]).astype(BF16)
        remote(mid.at[i], from_b.at[h], b_send.at[2 + h], b_recv.at[2 + h], to(0, 1 - 2 * h))
    line[3] = strip(3)
    wait_bytes(from_b.at[0], b_recv.at[2])
    wait_bytes(from_b.at[1], b_recv.at[3])
    fin[...] = total(line[3], from_b[0], from_b[1]).astype(BF16)

    def strips(n, _):
        other = lax.rem(z + n, 8)
        pltpu.make_async_remote_copy(src_ref=fin.at[:, pl.ds(pl.multiple_of(other * 32, 32), 32)], dst_ref=okv_ref.at[z],
                                     send_sem=z_send.at[2], recv_sem=z_recv.at[2], device_id={"head": other},
                                     device_id_type=MESH).start()
        return 0
    lax.fori_loop(1, 8, strips, 0)
    own_k = pltpu.make_async_copy(fin.at[:, pl.ds(pl.multiple_of(z * 32, 32), 32)], okv_ref.at[z], own_sem.at[2])
    own_k.start()
    rows(1)
    own_r = pltpu.make_async_copy(dz.at[me], oq_ref.at[me], own_sem.at[1])
    own_r.start()
    for c in started:
        c.wait_send()
    for h in range(2):
        wait_bytes(dz.at[pl.ds(0, 16), pl.ds(0, 7)], z_send.at[h])
    wait_bytes(oq_ref.at[pl.ds(0, NB - 1)], x_send.at[0])
    wait_bytes(oq_ref.at[pl.ds(0, NB - 1)], x_recv.at[0])
    wait_bytes(okv_ref.at[pl.ds(0, 7)], z_send.at[2])
    wait_bytes(okv_ref.at[pl.ds(0, 7)], z_recv.at[2])
    own_r.wait()
    own_k.wait()


def collect(dq, dkv):
    vm = pl.BlockSpec(memory_space=pltpu.VMEM)
    dma = pltpu.SemaphoreType.DMA
    block = (2, RB, HD)
    return pl.pallas_call(
        collect_kernel,
        out_shape=(jax.ShapeDtypeStruct((NB, 8, 8, HD), BF16), jax.ShapeDtypeStruct((8, 2, 32, HD), BF16)),
        in_specs=[vm] * 2, out_specs=(vm,) * 2,
        scratch_shapes=[
            pltpu.VMEM((16,) + block, BF16), pltpu.VMEM((3, 4) + block, BF16), pltpu.VMEM((2, 4) + block, BF16),
            pltpu.VMEM((2, 4, RB, HD), BF16), pltpu.VMEM((4,) + block, F32), pltpu.VMEM((2,) + block, BF16),
            pltpu.VMEM((2, RB, HD), BF16), pltpu.VMEM((3,) + block, BF16), pltpu.VMEM(block, BF16),
            pltpu.VMEM((NB, 8, 8, HD), BF16),
            dma((16,)), dma((16,)), dma((16,)), dma((16,)), dma((4,)), dma((4,)), dma((3,)), dma((3,)), dma((1,)), dma((1,)),
            dma((3,))],
        compiler_params=pltpu.CompilerParams(collective_id=1, has_side_effects=True, vmem_limit_bytes=40 << 20),
        name="collect",
    )(dq, dkv)


OI = ("outer", "inner")


def body(query, keys, values, forward_output, d_out, span_order):
    delta = jnp.sum(d_out.astype(F32) * forward_output.astype(F32), axis=-1)
    delta = jnp.transpose(delta.reshape(8, NB, 8), (1, 0, 2)).reshape(NB, 1, PIECE)
    delta = jnp.pad(delta, ((0, 0), (0, 0), (0, 128 - PIECE)))
    own_kv = jnp.stack([keys.reshape(RB, HD), values.reshape(RB, HD)])
    own_rows = jnp.stack([query, d_out]).reshape(2, 8, NB, 8, HD)
    kv, q, do, dl = spread(own_kv, own_rows, delta)
    dq, dkv = grads(span_order, q, do, dl, kv)
    oq, okv = collect(dq.reshape(NB, 8, 8, HD), dkv)
    okv = jnp.transpose(okv, (1, 2, 0, 3))
    return oq.reshape(1, 32, 64, HD), okv[0][None], okv[1][None]


def solution(mesh):
    rows = P(OI, "head", None)
    out = P(OI, "head", None, None)
    return jax.shard_map(body, mesh=mesh, in_specs=(rows,) * 5 + (P(),), out_specs=(out,) * 3, check_vma=False)
```
